512 devices in a mesh: subj: 16 (over z_lo, x, core), obj: 32 (over z_hi, y).
Axes of the slice: x: 4, y: 8, z: 8 (z_hi: 4, z_lo: 2; z = z_hi * 2 + z_lo), core: 2. Of those that a mesh axis runs over, the one named last changes fastest.
Arguments:
- subject_factors: bfloat16 [8192, 512], P(('subj', 'obj')), may hold values from -6 to 6
- object_factors: bfloat16 [16384, 512], P(('obj', 'subj')), may hold values from -6 to 6
- relations: bfloat16 [2, 512, 512], P(None, 'subj', 'obj'), may hold values from -0.01171875 to 0.01171875
- labels: int32 [2, 8192, 16384], P(None, 'subj', 'obj'), may hold values from 0 to 2
Outputs:
- grad_subject: float32 [8192, 512], P(('subj', 'obj'))
- grad_object: float32 [16384, 512], P(('obj', 'subj'))
- grad_relations: float32 [2, 512, 512], P(None, 'subj', 'obj')
- loss_rows: float32 [8192], P(('subj', 'obj'))
The draws below stay inside these ranges and needn't reach their ends.
All inputs are finite; a program needn't handle non-finite values.
Results may differ from the reference program's by a relative error of at most 0.02.
Values may be sent and summed in bfloat16 or wider, within the bound.
No kernel may reach another device: no remote copies, remote signals or barrier semaphores. Data moves between devices by JAX's collectives and lax.ppermute only.
A program may use at most 64 MiB of HBM per device.

```python
import jax
import jax.numpy as jnp
from jax import lax

RANK = 512
RELS = 2
SUB_DEV = 512
OBJ_DEV = 512
SUBJECTS = 8192
OBJECTS = 16384
N_SUBJ = 16
N_OBJ = 32


def with_ends(entries, key, least, largest):
    extent = entries.shape
    spot = [jax.random.randint(jax.random.fold_in(key, axis), (), 0, extent[axis]) for axis in range(len(extent))]
    entries = entries.at[tuple(spot)].set(least)
    longest = extent.index(max(extent))
    spot[longest] = (spot[longest] + 1) % extent[longest]
    return entries.at[tuple(spot)].set(largest)


def steps_of(rng, shape, split, smallest, top_value):
    loudness = 1.0
    for dim, shards_of in split:
        draws = jax.random.uniform(jax.random.fold_in(jax.random.fold_in(rng, 6), dim), (shards_of,), jnp.float32, smallest / len(split), top_value / len(split))
        loudness = loudness * jnp.repeat(jnp.exp(draws), shape[dim] // shards_of).reshape((-1,) + (1,) * (len(shape) - 1 - dim))
    return loudness


def bell_draw(rng, shape, deviation, reach, cuts=(), held_as=jnp.bfloat16):
    array = jax.random.normal(rng, shape, jnp.float32) * deviation
    if len(cuts) > 0:
        array = steps_of(rng, shape, cuts, -0.22, 0.18) * array
    return jnp.clip(array, min=-reach, max=reach).astype(held_as)


def setup_inputs(seed: int = 0) -> dict:
    keys = jax.random.split(jax.random.key(seed), 5)
    subject_factors = bell_draw(keys[0], (SUBJECTS, RANK), 1.0, 6.0, ((0, 512),))
    object_factors = bell_draw(keys[1], (OBJECTS, RANK), 1.0, 6.0, ((0, 512),))
    relations = bell_draw(keys[2], (RELS, RANK, RANK), (RANK * RANK) ** -0.5, 0.01171875, ((1, 16), (2, 32)))
    labels = with_ends(jax.random.randint(keys[3], (RELS, SUBJECTS, OBJECTS), 0, 3), jax.random.fold_in(keys[3], 1), 0, 2).astype(jnp.int32)
    return dict(subject_factors=subject_factors, object_factors=object_factors, relations=relations, labels=labels)


def reference(subject_factors, object_factors, relations, labels):
    subject_f = subject_factors.astype(jnp.float32)
    object_f = object_factors.astype(jnp.float32)
    relation_f = relations.astype(jnp.float32)
    left = jnp.einsum("ic,kca->kia", subject_f, relation_f).astype(jnp.bfloat16).astype(jnp.float32)
    right = jnp.einsum("jc,kac->kja", object_f, relation_f).astype(jnp.bfloat16).astype(jnp.float32)
    left_blocks = left.reshape(RELS, N_SUBJ, SUB_DEV, RANK)

    def per_block(carry, block):
        subject_acc, loss_acc, relation_acc = carry
        start = (block * OBJ_DEV).astype(jnp.int32)
        object_part = lax.dynamic_slice_in_dim(object_f, start, OBJ_DEV, 0)
        right_part = lax.dynamic_slice_in_dim(right, start, OBJ_DEV, 1)
        label_part = lax.dynamic_slice_in_dim(labels, start, OBJ_DEV, 2)
        scores = jnp.einsum("kia,ja->kij", left, object_part)
        target = (label_part == 2).astype(jnp.float32)
        weight = (label_part > 0).astype(jnp.float32)
        cell_loss = weight * (jax.nn.softplus(scores) - target * scores)
        residual = (weight * (jax.nn.sigmoid(scores) - target)).astype(jnp.bfloat16).astype(jnp.float32)
        loss_part = (jnp.sum(cell_loss, axis=(0, 2)) / (RELS * OBJECTS)).astype(jnp.bfloat16).astype(jnp.float32)
        subject_part = jnp.einsum("kij,kja->ia", residual, right_part).astype(jnp.bfloat16).astype(jnp.float32)
        residual_blocks = residual.reshape(RELS, N_SUBJ, SUB_DEV, OBJ_DEV)
        object_terms = jnp.einsum("knsj,knsa->nja", residual_blocks, left_blocks)
        object_grad = jnp.sum(object_terms.astype(jnp.bfloat16).astype(jnp.float32), axis=0)
        carried = jnp.einsum("kij,ja->kia", residual, object_part).astype(jnp.bfloat16).astype(jnp.float32)
        relation_part = jnp.einsum("ic,kia->kca", subject_f, carried)
        return (subject_acc + subject_part, loss_acc + loss_part, relation_acc + relation_part), object_grad

    start_carry = (jnp.zeros((SUBJECTS, RANK), jnp.float32), jnp.zeros((SUBJECTS,), jnp.float32),
                   jnp.zeros((RELS, RANK, RANK), jnp.float32))
    final, object_grads = lax.scan(per_block, start_carry, jnp.arange(N_OBJ, dtype=jnp.int32))
    subject_grad, loss_rows, relation_grad = final
    grad_object = object_grads.reshape(OBJECTS, RANK)
    return subject_grad, grad_object, relation_grad / SUBJECTS, loss_rows
```

```python
import jax
import jax.numpy as jnp
from jax import lax
from jax.experimental import pallas as pl
from jax.experimental.pallas import tpu as pltpu
from jax.sharding import PartitionSpec as P

F32 = jnp.float32
BF16 = jnp.bfloat16
LANES = 128
CHUNK = 128


def halves_to_lanes(rows):
    return jnp.concatenate([rows[:, :8], rows[:, 8:]], axis=2)


def lanes_to_halves(tile):
    half = tile.shape[2] // 2
    return jnp.concatenate([tile[:, :, :half], tile[:, :, half:]], axis=1)


def columns_to_rows(block):
    return jnp.concatenate(
        [block[:, c : c + LANES] for c in range(0, block.shape[1], LANES)], axis=0
    )


def dot(a, b, contract):
    return lax.dot_general(a, b, ((contract[:1], contract[1:]), ((), ())), preferred_element_type=F32)


def pack_subject(subject_ref, relation_ref, out_ref):
    copies, _, _ = out_ref.shape
    turned = jnp.concatenate([relation_ref[0], relation_ref[1]], axis=1).astype(F32)
    tile = halves_to_lanes(turned[None])[0].astype(BF16)
    factors = columns_to_rows(subject_ref[...])
    split = factors.shape[0]
    for p in range(copies):
        out_ref[p, :split] = factors
        out_ref[p, split:] = tile


def pack_object(gathered_ref, object_ref, out_ref):
    copies, _, width = out_ref.shape
    rows = object_ref.shape[0]
    split = gathered_ref.shape[1] - 8
    tiles = gathered_ref[:, split:, :].astype(F32)
    turned = lanes_to_halves(tiles)
    rel = turned.reshape(width, turned.shape[2]).T.astype(BF16)
    own = object_ref[...]
    for p in range(copies):
        out_ref[p, :rows] = own
        out_ref[p, rows:] = rel


def object_rows(gathered_ref, rows):
    part = gathered_ref[:, :rows, :]
    return part.reshape(-1, part.shape[2])


def relation_rows(gathered_ref, relation, rows):
    start = rows * (relation + 1)
    part = gathered_ref[:, start : start + rows, :]
    return part.reshape(-1, part.shape[2])


def grads(subject_ref, object_ref, labels_ref, out_ref, left_ref, carried_ref, residual_ref):
    relations, size, _ = labels_ref.shape
    rows = size // out_ref.shape[0]
    owners = subject_ref.shape[0]
    per_owner = size // owners
    subject = jnp.concatenate(
        [
            subject_ref[:, c * per_owner : (c + 1) * per_owner, :].reshape(size, LANES)
            for c in range(size // LANES)
        ],
        axis=1,
    )
    objects = object_rows(object_ref, rows)
    for k in range(relations):
        rel = relation_rows(object_ref, k, rows)
        left_ref[k] = dot(subject, rel, (1, 0)).astype(BF16)
        for at in range(0, size, CHUNK):
            span = pl.ds(at, CHUNK)
            scores = dot(left_ref[k, span], objects, (1, 1))
            codes = labels_ref[k, span]
            small = jnp.exp(-jnp.abs(scores))
            scale = 1.0 / (1.0 + small)
            sigmoid = jnp.where(scores >= 0.0, scale, small * scale)
            target = jnp.where(codes == 2, 1.0, 0.0)
            residual = jnp.where(codes > 0, sigmoid - target, 0.0).astype(BF16)
            residual_ref[k, span] = residual
            carried_ref[k, span] = dot(residual, objects, (1, 0)).astype(BF16)
        grad = dot(subject, carried_ref[k], (0, 0)).astype(BF16)
        out_ref[:, rows * (k + 1) : rows * (k + 2), :] = grad.reshape(-1, rows, size)
    grad_object = dot(residual_ref[0], left_ref[0], (0, 0))
    for k in range(1, relations):
        grad_object = grad_object + dot(residual_ref[k], left_ref[k], (0, 0))
    out_ref[:, :rows, :] = grad_object.astype(BF16).reshape(-1, rows, size)


def subject_grads(object_ref, labels_ref, left_ref, carried_ref, out_ref, *, total):
    relations, size, _ = labels_ref.shape
    rows = size // object_ref.shape[0]
    owners = out_ref.shape[0]
    per_owner = size // owners
    objects = object_rows(object_ref, rows)
    here = CHUNK // per_owner
    for at in range(0, size, CHUNK):
        span = pl.ds(at, CHUNK)
        loss = jnp.zeros((CHUNK, 1), F32)
        grad = jnp.zeros((CHUNK, size), F32)
        for k in range(relations):
            scores = dot(left_ref[k, span], objects, (1, 1))
            codes = labels_ref[k, span]
            soft = jnp.maximum(scores, 0.0) + jnp.log1p(jnp.exp(-jnp.abs(scores)))
            cell = jnp.where(codes == 2, soft - scores, soft)
            loss = loss + jnp.sum(jnp.where(codes > 0, cell, 0.0), axis=1, keepdims=True)
            grad = grad + dot(carried_ref[k, span], relation_rows(object_ref, k, rows), (1, 1))
        first = at // per_owner
        grad = grad.astype(BF16).reshape(here, per_owner, size)
        for c in range(size // LANES):
            out_ref[first : first + here, c * per_owner : (c + 1) * per_owner, :] = grad[
                :, :, c * LANES : (c + 1) * LANES
            ]
        part = jnp.broadcast_to(loss / total, (CHUNK, LANES // 2)).reshape(here, per_owner, -1)
        split = size // LANES * per_owner
        out_ref[first : first + here, split : split + 8, :] = halves_to_lanes(part).astype(BF16)


def sum_object(partial_ref, subject_ref, grad_ref, out_ref):
    rows = grad_ref.shape[0]
    width = grad_ref.shape[1]
    total = jnp.sum(partial_ref[...].astype(F32), axis=0)
    grad_ref[...] = total[:rows]
    turned = total[rows:].T
    owners = subject_ref.shape[0]
    tiles = halves_to_lanes(turned.reshape(owners, width // owners, -1)).astype(BF16)
    split = subject_ref.shape[1]
    out_ref[:, :split, :] = subject_ref[...]
    out_ref[:, split:, :] = tiles


def sum_subject(partial_ref, grad_ref, relation_ref, loss_ref, *, total):
    rows, width = grad_ref.shape
    summed = jnp.sum(partial_ref[...].astype(F32), axis=0)
    blocks = width // LANES
    grad_ref[...] = jnp.concatenate(
        [summed[c * rows : (c + 1) * rows] for c in range(blocks)], axis=1
    )
    at = blocks * rows
    loss = lanes_to_halves(summed[None, at : at + 8])[0]
    loss_ref[...] = loss.T[:1]
    turned = lanes_to_halves(summed[None, at + 8 : at + 16])[0] * (1.0 / total)
    columns = relation_ref.shape[2]
    for k in range(relation_ref.shape[0]):
        relation_ref[k] = turned[:, k * columns : (k + 1) * columns]


def shape(dims, dtype=BF16):
    return jax.ShapeDtypeStruct(dims, dtype)


def call(kernel, name, outs, *args, scratch=()):
    return pl.pallas_call(kernel, out_shape=outs, scratch_shapes=scratch, name=name)(*args)


def body(subject_factors, object_factors, relations, labels):
    subj, obj = lax.axis_size("subj"), lax.axis_size("obj")
    subject_rows, width = subject_factors.shape
    object_part = object_factors.shape[0]
    count, rel_rows, rel_columns = relations.shape
    _, subjects, objects = labels.shape
    strips = width // LANES * subject_rows
    turned = jnp.swapaxes(relations, 1, 2)
    sent = call(pack_subject, "pack_subject", shape((obj, strips + 8, LANES)), subject_factors, turned)
    subject_all = lax.all_to_all(sent, "obj", 0, 0, tiled=True)
    stacked = object_part + count * rel_rows
    sent = call(
        pack_object, "pack_object", shape((subj, stacked, width)), subject_all, object_factors
    )
    object_all = lax.all_to_all(sent, "subj", 0, 0, tiled=True)
    square = (count, subjects, width)
    partial, left, carried = call(
        grads,
        "grads",
        (shape((subj, stacked, width)), shape(square), shape(square)),
        subject_all,
        object_all,
        labels,
        scratch=[pltpu.VMEM((count, subjects, objects), BF16)],
    )
    received = lax.all_to_all(partial, "subj", 0, 0, tiled=True)
    scale = float(count * objects * obj)
    packed = call(
        lambda *refs: subject_grads(*refs, total=scale),
        "subject_grads",
        shape((obj, strips + 8, LANES)),
        object_all,
        labels,
        left,
        carried,
    )
    grad_object, sent = call(
        sum_object,
        "sum_object",
        (shape((object_part, width), F32), shape((obj, strips + 16, LANES))),
        received,
        packed,
    )
    received = lax.all_to_all(sent, "obj", 0, 0, tiled=True)
    scale = float(subjects * subj)
    grad_subject, grad_relations, loss = call(
        lambda *refs: sum_subject(*refs, total=scale),
        "sum_subject",
        (
            shape((subject_rows, width), F32),
            shape((count, rel_columns, rel_rows), F32),
            shape((1, subject_rows), F32),
        ),
        received,
    )
    return grad_subject, grad_object, jnp.swapaxes(grad_relations, 1, 2), loss.reshape(subject_rows)


def solution(mesh):
    placed = (
        P(("subj", "obj"), None),
        P(("obj", "subj"), None),
        P(None, "subj", "obj"),
        P(None, "subj", "obj"),
    )
    return jax.shard_map(
        body,
        mesh=mesh,
        in_specs=placed,
        out_specs=(
            P(("subj", "obj"), None),
            P(("obj", "subj"), None),
            P(None, "subj", "obj"),
            P(("subj", "obj")),
        ),
        check_vma=False,
    )
```

```python
import jax
import jax.numpy as jnp
from jax import lax
from jax.experimental import pallas as pl
from jax.experimental.pallas import tpu as pltpu
from jax.sharding import Mesh
from jax.sharding import PartitionSpec as P

F32 = jnp.float32
BF16 = jnp.bfloat16
LANES = 128
CHUNK = 128


def halves_to_lanes(rows):
    return jnp.concatenate([rows[:, :8], rows[:, 8:]], axis=2)


def lanes_to_halves(tile):
    half = tile.shape[2] // 2
    return jnp.concatenate([tile[:, :, :half], tile[:, :, half:]], axis=1)


def columns_to_rows(block):
    return jnp.concatenate(
        [block[:, c : c + LANES] for c in range(0, block.shape[1], LANES)], axis=0
    )


def dot(a, b, contract):
    return lax.dot_general(a, b, ((contract[:1], contract[1:]), ((), ())), preferred_element_type=F32)


def pack_subject(subject_ref, relation_ref, out_ref):
    copies, _, _ = out_ref.shape
    turned = jnp.concatenate([relation_ref[0], relation_ref[1]], axis=1).astype(F32)
    tile = halves_to_lanes(turned[None])[0].astype(BF16)
    factors = columns_to_rows(subject_ref[...])
    split = factors.shape[0]
    for p in range(copies):
        out_ref[p, :split] = factors
        out_ref[p, split:] = tile


def pack_object(gathered_ref, object_ref, out_ref):
    copies, _, width = out_ref.shape
    rows = object_ref.shape[0]
    split = gathered_ref.shape[1] - 8
    tiles = gathered_ref[:, split:, :].astype(F32)
    turned = lanes_to_halves(tiles)
    rel = turned.reshape(width, turned.shape[2]).T.astype(BF16)
    own = object_ref[...]
    for p in range(copies):
        out_ref[p, :rows] = own
        out_ref[p, rows:] = rel


def stacked_rows(own_ref, other_ref, part, rows):
    first = lax.axis_index("core") == 0
    own = own_ref[:, rows * part : rows * (part + 1), :]
    other = other_ref[:, rows * part : rows * (part + 1), :]
    even = jnp.where(first, own, other)
    odd = jnp.where(first, other, own)
    return jnp.stack([even, odd], axis=1).reshape(-1, own.shape[2])


def store_owners(keep_ref, send_ref, part, rows, values):
    first = lax.axis_index("core") == 0
    by_core = values.reshape(keep_ref.shape[0], 2, rows, values.shape[1])
    even, odd = by_core[:, 0], by_core[:, 1]
    span = slice(rows * part, rows * (part + 1))
    keep_ref[:, span, :] = jnp.where(first, even, odd).astype(BF16)
    send_ref[:, span, :] = jnp.where(first, odd, even).astype(BF16)


def grads(
    subject_ref,
    own_ref,
    other_ref,
    labels_ref,
    keep_ref,
    send_ref,
    left_ref,
    carried_ref,
    residual_ref,
):
    relations, size, _ = labels_ref.shape
    rows = size // (2 * keep_ref.shape[0])
    owners = subject_ref.shape[0]
    per_owner = size // owners
    subject = jnp.concatenate(
        [
            subject_ref[:, c * per_owner : (c + 1) * per_owner, :].reshape(size, LANES)
            for c in range(size // LANES)
        ],
        axis=1,
    )
    objects = stacked_rows(own_ref, other_ref, 0, rows)
    for k in range(relations):
        rel = stacked_rows(own_ref, other_ref, k + 1, rows)
        left_ref[k] = dot(subject, rel, (1, 0)).astype(BF16)
        for at in range(0, size, CHUNK):
            span = pl.ds(at, CHUNK)
            scores = dot(left_ref[k, span], objects, (1, 1))
            codes = labels_ref[k, span]
            small = jnp.exp(-jnp.abs(scores))
            scale = 1.0 / (1.0 + small)
            sigmoid = jnp.where(scores >= 0.0, scale, small * scale)
            target = jnp.where(codes == 2, 1.0, 0.0)
            residual = jnp.where(codes > 0, sigmoid - target, 0.0).astype(BF16)
            residual_ref[k, span] = residual
            carried_ref[k, span] = dot(residual, objects, (1, 0)).astype(BF16)
        store_owners(keep_ref, send_ref, k + 1, rows, dot(subject, carried_ref[k], (0, 0)))
    grad_object = dot(residual_ref[0], left_ref[0], (0, 0))
    for k in range(1, relations):
        grad_object = grad_object + dot(residual_ref[k], left_ref[k], (0, 0))
    store_owners(keep_ref, send_ref, 0, rows, grad_object)


def add_pair(keep_ref, received_ref, out_ref):
    out_ref[...] = (keep_ref[...].astype(F32) + received_ref[...].astype(F32)).astype(BF16)


def subject_grads(own_ref, other_ref, labels_ref, left_ref, carried_ref, out_ref, *, total):
    relations, size, _ = labels_ref.shape
    rows = size // (2 * own_ref.shape[0])
    owners = out_ref.shape[0]
    per_owner = size // owners
    objects = stacked_rows(own_ref, other_ref, 0, rows)
    rels = [stacked_rows(own_ref, other_ref, k + 1, rows) for k in range(relations)]
    here = CHUNK // per_owner
    for at in range(0, size, CHUNK):
        span = pl.ds(at, CHUNK)
        loss = jnp.zeros((CHUNK, 1), F32)
        grad = jnp.zeros((CHUNK, size), F32)
        for k in range(relations):
            scores = dot(left_ref[k, span], objects, (1, 1))
            codes = labels_ref[k, span]
            soft = jnp.maximum(scores, 0.0) + jnp.log1p(jnp.exp(-jnp.abs(scores)))
            cell = jnp.where(codes == 2, soft - scores, soft)
            loss = loss + jnp.sum(jnp.where(codes > 0, cell, 0.0), axis=1, keepdims=True)
            grad = grad + dot(carried_ref[k, span], rels[k], (1, 1))
        first = at // per_owner
        grad = grad.astype(BF16).reshape(here, per_owner, size)
        for c in range(size // LANES):
            out_ref[first : first + here, c * per_owner : (c + 1) * per_owner, :] = grad[
                :, :, c * LANES : (c + 1) * LANES
            ]
        part = jnp.broadcast_to(loss / total, (CHUNK, LANES // 2)).reshape(here, per_owner, -1)
        split = size // LANES * per_owner
        out_ref[first : first + here, split : split + 8, :] = halves_to_lanes(part).astype(BF16)


def sum_object(partial_ref, subject_ref, grad_ref, out_ref):
    rows = grad_ref.shape[0]
    width = grad_ref.shape[1]
    total = jnp.sum(partial_ref[...].astype(F32), axis=0)
    grad_ref[...] = total[:rows]
    turned = total[rows:].T
    owners = subject_ref.shape[0]
    tiles = halves_to_lanes(turned.reshape(owners, width // owners, -1)).astype(BF16)
    split = subject_ref.shape[1]
    out_ref[:, :split, :] = subject_ref[...]
    out_ref[:, split:, :] = tiles


def sum_subject(partial_ref, grad_ref, relation_ref, loss_ref, *, total):
    rows, width = grad_ref.shape
    summed = jnp.sum(partial_ref[...].astype(F32), axis=0)
    blocks = width // LANES
    grad_ref[...] = jnp.concatenate(
        [summed[c * rows : (c + 1) * rows] for c in range(blocks)], axis=1
    )
    at = blocks * rows
    loss = lanes_to_halves(summed[None, at : at + 8])[0]
    loss_ref[...] = loss.T[:1]
    turned = lanes_to_halves(summed[None, at + 8 : at + 16])[0] * (1.0 / total)
    columns = relation_ref.shape[2]
    for k in range(relation_ref.shape[0]):
        relation_ref[k] = turned[:, k * columns : (k + 1) * columns]


def shape(dims, dtype=BF16):
    return jax.ShapeDtypeStruct(dims, dtype)


def call(kernel, name, outs, *args, scratch=()):
    return pl.pallas_call(kernel, out_shape=outs, scratch_shapes=scratch, name=name)(*args)


def to_other_core(array):
    return lax.ppermute(array, "core", [(0, 1), (1, 0)])


def body(subject_factors, object_factors, relations, labels):
    chips, obj = lax.axis_size("chip"), lax.axis_size("obj")
    subj = 2 * chips
    subject_rows, width = subject_factors.shape
    object_part = object_factors.shape[0]
    count, rel_rows, rel_columns = relations.shape
    _, subjects, objects = labels.shape
    strips = width // LANES * subject_rows
    turned = jnp.swapaxes(relations, 1, 2)
    sent = call(pack_subject, "pack_subject", shape((obj, strips + 8, LANES)), subject_factors, turned)
    subject_all = lax.all_to_all(sent, "obj", 0, 0, tiled=True)
    stacked = (chips, object_part + count * rel_rows, width)
    sent = call(pack_object, "pack_object", shape(stacked), subject_all, object_factors)
    own = lax.all_to_all(sent, "chip", 0, 0, tiled=True)
    other = to_other_core(own)
    square = (count, subjects, width)
    keep, send, left, carried = call(
        grads,
        "grads",
        (shape(stacked), shape(stacked), shape(square), shape(square)),
        subject_all,
        own,
        other,
        labels,
        scratch=[pltpu.VMEM((count, subjects, objects), BF16)],
    )
    sent = call(add_pair, "add_pair", shape(stacked), keep, to_other_core(send))
    received = lax.all_to_all(sent, "chip", 0, 0, tiled=True)
    scale = float(count * objects * obj)
    packed = call(
        lambda *refs: subject_grads(*refs, total=scale),
        "subject_grads",
        shape((obj, strips + 8, LANES)),
        own,
        other,
        labels,
        left,
        carried,
    )
    grad_object, sent = call(
        sum_object,
        "sum_object",
        (shape((object_part, width), F32), shape((obj, strips + 16, LANES))),
        received,
        packed,
    )
    received = lax.all_to_all(sent, "obj", 0, 0, tiled=True)
    scale = float(subjects * subj)
    grad_subject, grad_relations, loss = call(
        lambda *refs: sum_subject(*refs, total=scale),
        "sum_subject",
        (
            shape((subject_rows, width), F32),
            shape((count, rel_columns, rel_rows), F32),
            shape((1, subject_rows), F32),
        ),
        received,
    )
    return grad_subject, grad_object, jnp.swapaxes(grad_relations, 1, 2), loss.reshape(subject_rows)


def solution(mesh):
    subj, obj = mesh.shape["subj"], mesh.shape["obj"]
    cores = Mesh(mesh.devices.reshape(subj // 2, 2, obj), ("chip", "core", "obj"))
    rows = ("chip", "core")
    placed = (
        P((*rows, "obj"), None),
        P(("obj", *rows), None),
        P(None, rows, "obj"),
        P(None, rows, "obj"),
    )
    return jax.shard_map(
        body,
        mesh=cores,
        in_specs=placed,
        out_specs=(
            P((*rows, "obj"), None),
            P(("obj", *rows), None),
            P(None, rows, "obj"),
            P((*rows, "obj")),
        ),
        check_vma=False,
    )
```

```python
import jax
import jax.numpy as jnp
from jax import lax
from jax.experimental import pallas as pl
from jax.experimental.pallas import tpu as pltpu
from jax.sharding import Mesh
from jax.sharding import PartitionSpec as P

F32 = jnp.float32
BF16 = jnp.bfloat16
LANES = 128
CHUNK = 128
GRANT = 20 * 2**20


def halves_to_lanes(rows):
    return jnp.concatenate([rows[:, :8], rows[:, 8:]], axis=2)


def lanes_to_halves(tile):
    half = tile.shape[2] // 2
    return jnp.concatenate([tile[:, :, :half], tile[:, :, half:]], axis=1)


def columns_to_rows(block):
    return jnp.concatenate(
        [block[:, c : c + LANES] for c in range(0, block.shape[1], LANES)], axis=0
    )


def dot(a, b, contract):
    return lax.dot_general(a, b, ((contract[:1], contract[1:]), ((), ())), preferred_element_type=F32)


def pack_subject(subject_ref, relation_ref, out_ref):
    copies, _, _ = out_ref.shape
    turned = jnp.concatenate([relation_ref[0], relation_ref[1]], axis=1).astype(F32)
    tile = halves_to_lanes(turned[None])[0].astype(BF16)
    factors = columns_to_rows(subject_ref[...])
    split = factors.shape[0]
    for p in range(copies):
        out_ref[p, :split] = factors
        out_ref[p, split:] = tile


def pack_object(gathered_ref, object_ref, out_ref):
    copies, _, width = out_ref.shape
    rows = object_ref.shape[0]
    split = gathered_ref.shape[1] - 8
    tiles = gathered_ref[:, split:, :].astype(F32)
    turned = lanes_to_halves(tiles)
    rel = turned.reshape(width, turned.shape[2]).T.astype(BF16)
    own = object_ref[...]
    for p in range(copies):
        out_ref[p, :rows] = own
        out_ref[p, rows:] = rel


def stacked_rows(own_ref, other_ref, part, rows):
    first = lax.axis_index("core") == 0
    own = own_ref[:, rows * part : rows * (part + 1), :]
    other = other_ref[:, rows * part : rows * (part + 1), :]
    even = jnp.where(first, own, other)
    odd = jnp.where(first, other, own)
    return jnp.stack([even, odd], axis=1).reshape(-1, own.shape[2])


def store_owners(keep_ref, send_ref, part, rows, values):
    first = lax.axis_index("core") == 0
    by_core = values.reshape(keep_ref.shape[0], 2, rows, values.shape[1])
    even, odd = by_core[:, 0], by_core[:, 1]
    span = slice(rows * part, rows * (part + 1))
    keep_ref[:, span, :] = jnp.where(first, even, odd).astype(BF16)
    send_ref[:, span, :] = jnp.where(first, odd, even).astype(BF16)


def grads(
    subject_ref,
    own_ref,
    other_ref,
    labels_ref,
    keep_ref,
    send_ref,
    left_ref,
    carried_ref,
    residual_ref,
):
    relations, size, _ = labels_ref.shape
    rows = size // (2 * keep_ref.shape[0])
    owners = subject_ref.shape[0]
    per_owner = size // owners
    subject = jnp.concatenate(
        [
            subject_ref[:, c * per_owner : (c + 1) * per_owner, :].reshape(size, LANES)
            for c in range(size // LANES)
        ],
        axis=1,
    )
    objects = stacked_rows(own_ref, other_ref, 0, rows)
    for k in range(relations):
        rel = stacked_rows(own_ref, other_ref, k + 1, rows)
        left_ref[k] = dot(subject, rel, (1, 0)).astype(BF16)
        for at in range(0, size, CHUNK):
            span = pl.ds(at, CHUNK)
            scores = dot(left_ref[k, span], objects, (1, 1))
            codes = labels_ref[k, span]
            small = jnp.exp(-jnp.abs(scores))
            scale = 1.0 / (1.0 + small)
            sigmoid = jnp.where(scores >= 0.0, scale, small * scale)
            target = jnp.where(codes == 2, 1.0, 0.0)
            residual = jnp.where(codes > 0, sigmoid - target, 0.0).astype(BF16)
            residual_ref[k, span] = residual
            carried_ref[k, span] = dot(residual, objects, (1, 0)).astype(BF16)
        store_owners(keep_ref, send_ref, k + 1, rows, dot(subject, carried_ref[k], (0, 0)))
    grad_object = dot(residual_ref[0], left_ref[0], (0, 0))
    for k in range(1, relations):
        grad_object = grad_object + dot(residual_ref[k], left_ref[k], (0, 0))
    store_owners(keep_ref, send_ref, 0, rows, grad_object)


def add_pair(keep_ref, received_ref, out_ref):
    out_ref[...] = (keep_ref[...].astype(F32) + received_ref[...].astype(F32)).astype(BF16)


def subject_grads(own_ref, other_ref, labels_ref, left_ref, carried_ref, out_ref, *, total):
    relations, size, _ = labels_ref.shape
    rows = size // (2 * own_ref.shape[0])
    owners = out_ref.shape[0]
    per_owner = size // owners
    objects = stacked_rows(own_ref, other_ref, 0, rows)
    rels = [stacked_rows(own_ref, other_ref, k + 1, rows) for k in range(relations)]
    here = CHUNK // per_owner
    for at in range(0, size, CHUNK):
        span = pl.ds(at, CHUNK)
        loss = jnp.zeros((CHUNK, 1), F32)
        grad = jnp.zeros((CHUNK, size), F32)
        for k in range(relations):
            scores = dot(left_ref[k, span], objects, (1, 1))
            codes = labels_ref[k, span]
            soft = jnp.maximum(scores, 0.0) + jnp.log1p(jnp.exp(-jnp.abs(scores)))
            cell = jnp.where(codes == 2, soft - scores, soft)
            loss = loss + jnp.sum(jnp.where(codes > 0, cell, 0.0), axis=1, keepdims=True)
            grad = grad + dot(carried_ref[k, span], rels[k], (1, 1))
        first = at // per_owner
        grad = grad.astype(BF16).reshape(here, per_owner, size)
        for c in range(size // LANES):
            out_ref[first : first + here, c * per_owner : (c + 1) * per_owner, :] = grad[
                :, :, c * LANES : (c + 1) * LANES
            ]
        part = jnp.broadcast_to(loss / total, (CHUNK, LANES // 2)).reshape(here, per_owner, -1)
        split = size // LANES * per_owner
        out_ref[first : first + here, split : split + 8, :] = halves_to_lanes(part).astype(BF16)


def sum_object(partial_ref, subject_ref, grad_ref, out_ref):
    rows = grad_ref.shape[0]
    width = grad_ref.shape[1]
    total = jnp.sum(partial_ref[...].astype(F32), axis=0)
    grad_ref[...] = total[:rows]
    turned = total[rows:].T
    owners = subject_ref.shape[0]
    tiles = halves_to_lanes(turned.reshape(owners, width // owners, -1)).astype(BF16)
    split = subject_ref.shape[1]
    out_ref[:, :split, :] = subject_ref[...]
    out_ref[:, split:, :] = tiles


def sum_subject(partial_ref, grad_ref, relation_ref, loss_ref, *, total):
    rows, width = grad_ref.shape
    summed = jnp.sum(partial_ref[...].astype(F32), axis=0)
    blocks = width // LANES
    grad_ref[...] = jnp.concatenate(
        [summed[c * rows : (c + 1) * rows] for c in range(blocks)], axis=1
    )
    at = blocks * rows
    loss = lanes_to_halves(summed[None, at : at + 8])[0]
    loss_ref[...] = loss.T[:1]
    turned = lanes_to_halves(summed[None, at + 8 : at + 16])[0] * (1.0 / total)
    columns = relation_ref.shape[2]
    for k in range(relation_ref.shape[0]):
        relation_ref[k] = turned[:, k * columns : (k + 1) * columns]


def shape(dims, dtype=BF16):
    return jax.ShapeDtypeStruct(dims, dtype)


def call(kernel, name, outs, *args, scratch=()):
    return pl.pallas_call(
        kernel,
        out_shape=outs,
        scratch_shapes=scratch,
        name=name,
        compiler_params=pltpu.CompilerParams(vmem_limit_bytes=GRANT),
    )(*args)


def to_other_core(array):
    return lax.ppermute(array, "core", [(0, 1), (1, 0)])


def body(subject_factors, object_factors, relations, labels):
    chips, obj = lax.axis_size("chip"), lax.axis_size("obj")
    subj = 2 * chips
    subject_rows, width = subject_factors.shape
    object_part = object_factors.shape[0]
    count, rel_rows, rel_columns = relations.shape
    _, subjects, objects = labels.shape
    strips = width // LANES * subject_rows
    turned = jnp.swapaxes(relations, 1, 2)
    sent = call(pack_subject, "pack_subject", shape((obj, strips + 8, LANES)), subject_factors, turned)
    subject_all = lax.all_to_all(sent, "obj", 0, 0, tiled=True)
    stacked = (chips, object_part + count * rel_rows, width)
    sent = call(pack_object, "pack_object", shape(stacked), subject_all, object_factors)
    own = lax.all_to_all(sent, "chip", 0, 0, tiled=True)
    other = to_other_core(own)
    square = (count, subjects, width)
    keep, send, left, carried = call(
        grads,
        "grads",
        (shape(stacked), shape(stacked), shape(square), shape(square)),
        subject_all,
        own,
        other,
        labels,
        scratch=[pltpu.VMEM((count, subjects, objects), BF16)],
    )
    sent = call(add_pair, "add_pair", shape(stacked), keep, to_other_core(send))
    received = lax.all_to_all(sent, "chip", 0, 0, tiled=True)
    scale = float(count * objects * obj)
    packed = call(
        lambda *refs: subject_grads(*refs, total=scale),
        "subject_grads",
        shape((obj, strips + 8, LANES)),
        own,
        other,
        labels,
        left,
        carried,
    )
    grad_object, sent = call(
        sum_object,
        "sum_object",
        (shape((object_part, width), F32), shape((obj, strips + 16, LANES))),
        received,
        packed,
    )
    received = lax.all_to_all(sent, "obj", 0, 0, tiled=True)
    scale = float(subjects * subj)
    grad_subject, grad_relations, loss = call(
        lambda *refs: sum_subject(*refs, total=scale),
        "sum_subject",
        (
            shape((subject_rows, width), F32),
            shape((count, rel_columns, rel_rows), F32),
            shape((1, subject_rows), F32),
        ),
        received,
    )
    return grad_subject, grad_object, jnp.swapaxes(grad_relations, 1, 2), loss.reshape(subject_rows)


def solution(mesh):
    subj, obj = mesh.shape["subj"], mesh.shape["obj"]
    cores = Mesh(mesh.devices.reshape(subj // 2, 2, obj), ("chip", "core", "obj"))
    rows = ("chip", "core")
    placed = (
        P((*rows, "obj"), None),
        P(("obj", *rows), None),
        P(None, rows, "obj"),
        P(None, rows, "obj"),
    )
    return jax.shard_map(
        body,
        mesh=cores,
        in_specs=placed,
        out_specs=(
            P((*rows, "obj"), None),
            P(("obj", *rows), None),
            P(None, rows, "obj"),
            P((*rows, "obj")),
        ),
        check_vma=False,
    )
```

```python
import jax
import jax.numpy as jnp
from jax import lax
from jax.experimental import pallas as pl
from jax.experimental.pallas import tpu as pltpu
from jax.sharding import Mesh
from jax.sharding import PartitionSpec as P

F32 = jnp.float32
BF16 = jnp.bfloat16
LANES = 128
CHUNK = 128
GRANT = 20 * 2**20


def halves_to_lanes(rows):
    return jnp.concatenate([rows[:, :8], rows[:, 8:]], axis=2)


def lanes_to_halves(tile):
    half = tile.shape[2] // 2
    return jnp.concatenate([tile[:, :, :half], tile[:, :, half:]], axis=1)


def columns_to_rows(block):
    return jnp.concatenate(
        [block[:, c : c + LANES] for c in range(0, block.shape[1], LANES)], axis=0
    )


def dot(a, b, contract):
    return lax.dot_general(a, b, ((contract[:1], contract[1:]), ((), ())), preferred_element_type=F32)


def pack_subject(
    subject_hbm, relation_hbm, object_hbm, out_ref, object_ref, subject_ref, relation_ref, arrived
):
    copies, _, _ = out_ref.shape
    loads = [
        pltpu.make_async_copy(subject_hbm, subject_ref, arrived.at[0]),
        pltpu.make_async_copy(relation_hbm, relation_ref, arrived.at[1]),
        pltpu.make_async_copy(object_hbm, object_ref, arrived.at[2]),
    ]
    for load in loads:
        load.start()
    for load in loads:
        load.wait()
    turned = jnp.concatenate([relation_ref[0], relation_ref[1]], axis=1).astype(F32)
    tile = halves_to_lanes(turned[None])[0].astype(BF16)
    factors = columns_to_rows(subject_ref[...])
    split = factors.shape[0]
    for p in range(copies):
        out_ref[p, :split] = factors
        out_ref[p, split:] = tile


def pack_object(gathered_ref, object_ref, out_ref):
    copies, _, width = out_ref.shape
    rows = object_ref.shape[0]
    split = gathered_ref.shape[1] - 8
    tiles = gathered_ref[:, split:, :].astype(F32)
    turned = lanes_to_halves(tiles)
    rel = turned.reshape(width, turned.shape[2]).T.astype(BF16)
    own = object_ref[...]
    for p in range(copies):
        out_ref[p, :rows] = own
        out_ref[p, rows:] = rel


def stacked_rows(own_ref, other_ref, part, rows):
    first = lax.axis_index("core") == 0
    own = own_ref[:, rows * part : rows * (part + 1), :]
    other = other_ref[:, rows * part : rows * (part + 1), :]
    even = jnp.where(first, own, other)
    odd = jnp.where(first, other, own)
    return jnp.stack([even, odd], axis=1).reshape(-1, own.shape[2])


def store_owners(keep_ref, send_ref, part, rows, values):
    first = lax.axis_index("core") == 0
    by_core = values.reshape(keep_ref.shape[0], 2, rows, values.shape[1])
    even, odd = by_core[:, 0], by_core[:, 1]
    span = slice(rows * part, rows * (part + 1))
    keep_ref[:, span, :] = jnp.where(first, even, odd).astype(BF16)
    send_ref[:, span, :] = jnp.where(first, odd, even).astype(BF16)


def grads(
    subject_ref,
    own_ref,
    other_ref,
    labels_ref,
    keep_ref,
    send_ref,
    carried_ref,
    scores_ref,
    left_ref,
    residual_ref,
):
    relations, size, _ = labels_ref.shape
    rows = size // (2 * keep_ref.shape[0])
    owners = subject_ref.shape[0]
    per_owner = size // owners
    subject = jnp.concatenate(
        [
            subject_ref[:, c * per_owner : (c + 1) * per_owner, :].reshape(size, LANES)
            for c in range(size // LANES)
        ],
        axis=1,
    )
    objects = stacked_rows(own_ref, other_ref, 0, rows)
    for k in range(relations):
        rel = stacked_rows(own_ref, other_ref, k + 1, rows)
        left_ref[k] = dot(subject, rel, (1, 0)).astype(BF16)
        for at in range(0, size, CHUNK):
            span = pl.ds(at, CHUNK)
            scores = dot(left_ref[k, span], objects, (1, 1))
            scores_ref[k, span] = scores
            codes = labels_ref[k, span]
            small = jnp.exp(-jnp.abs(scores))
            scale = 1.0 / (1.0 + small)
            sigmoid = jnp.where(scores >= 0.0, scale, small * scale)
            target = jnp.where(codes == 2, 1.0, 0.0)
            residual = jnp.where(codes > 0, sigmoid - target, 0.0).astype(BF16)
            residual_ref[k, span] = residual
            carried_ref[k, span] = dot(residual, objects, (1, 0)).astype(BF16)
        store_owners(keep_ref, send_ref, k + 1, rows, dot(subject, carried_ref[k], (0, 0)))
    grad_object = dot(residual_ref[0], left_ref[0], (0, 0))
    for k in range(1, relations):
        grad_object = grad_object + dot(residual_ref[k], left_ref[k], (0, 0))
    store_owners(keep_ref, send_ref, 0, rows, grad_object)


def add_pair(keep_ref, received_ref, _, out_ref):
    out_ref[...] = (keep_ref[...].astype(F32) + received_ref[...].astype(F32)).astype(BF16)


def subject_grads(own_ref, other_ref, labels_ref, scores_ref, carried_ref, out_ref, *, total):
    relations, size, _ = labels_ref.shape
    rows = size // (2 * own_ref.shape[0])
    owners = out_ref.shape[0]
    per_owner = size // owners
    rels = [stacked_rows(own_ref, other_ref, k + 1, rows) for k in range(relations)]
    here = CHUNK // per_owner
    for at in range(0, size, CHUNK):
        span = pl.ds(at, CHUNK)
        loss = jnp.zeros((CHUNK, 1), F32)
        grad = jnp.zeros((CHUNK, size), F32)
        for k in range(relations):
            scores = scores_ref[k, span]
            codes = labels_ref[k, span]
            soft = jnp.maximum(scores, 0.0) + jnp.log1p(jnp.exp(-jnp.abs(scores)))
            cell = jnp.where(codes == 2, soft - scores, soft)
            loss = loss + jnp.sum(jnp.where(codes > 0, cell, 0.0), axis=1, keepdims=True)
            grad = grad + dot(carried_ref[k, span], rels[k], (1, 1))
        first = at // per_owner
        grad = grad.astype(BF16).reshape(here, per_owner, size)
        for c in range(size // LANES):
            out_ref[first : first + here, c * per_owner : (c + 1) * per_owner, :] = grad[
                :, :, c * LANES : (c + 1) * LANES
            ]
        part = jnp.broadcast_to(loss / total, (CHUNK, LANES // 2)).reshape(here, per_owner, -1)
        split = size // LANES * per_owner
        out_ref[first : first + here, split : split + 8, :] = halves_to_lanes(part).astype(BF16)


def sum_object(partial_ref, subject_ref, grad_ref, out_ref):
    rows = grad_ref.shape[0]
    width = grad_ref.shape[1]
    total = jnp.sum(partial_ref[...].astype(F32), axis=0)
    grad_ref[...] = total[:rows]
    turned = total[rows:].T
    owners = subject_ref.shape[0]
    tiles = halves_to_lanes(turned.reshape(owners, width // owners, -1)).astype(BF16)
    split = subject_ref.shape[1]
    out_ref[:, :split, :] = subject_ref[...]
    out_ref[:, split:, :] = tiles


def sum_subject(partial_ref, grad_ref, relation_ref, loss_ref, *, total):
    rows, width = grad_ref.shape
    summed = jnp.sum(partial_ref[...].astype(F32), axis=0)
    blocks = width // LANES
    grad_ref[...] = jnp.concatenate(
        [summed[c * rows : (c + 1) * rows] for c in range(blocks)], axis=1
    )
    at = blocks * rows
    loss = lanes_to_halves(summed[None, at : at + 8])[0]
    loss_ref[...] = loss.T[:1]
    turned = lanes_to_halves(summed[None, at + 8 : at + 16])[0] * (1.0 / total)
    columns = relation_ref.shape[2]
    for k in range(relation_ref.shape[0]):
        relation_ref[k] = turned[:, k * columns : (k + 1) * columns]


def shape(dims, dtype=BF16):
    return jax.ShapeDtypeStruct(dims, dtype)


def call(kernel, name, outs, *args, scratch=(), spaces=None):
    spaces = spaces or [None] * len(args)
    args = [
        pltpu.with_memory_space_constraint(a, s) if s is pltpu.HBM else a
        for a, s in zip(args, spaces)
    ]
    return pl.pallas_call(
        kernel,
        out_shape=outs,
        in_specs=[pl.BlockSpec(memory_space=space) for space in spaces],
        scratch_shapes=scratch,
        name=name,
        compiler_params=pltpu.CompilerParams(vmem_limit_bytes=GRANT),
    )(*args)


def to_other_core(array):
    return lax.ppermute(array, "core", [(0, 1), (1, 0)])


def body(subject_factors, object_factors, relations, labels):
    chips, obj = lax.axis_size("chip"), lax.axis_size("obj")
    subj = 2 * chips
    subject_rows, width = subject_factors.shape
    object_part = object_factors.shape[0]
    count, rel_rows, rel_columns = relations.shape
    _, subjects, objects = labels.shape
    strips = width // LANES * subject_rows
    turned = jnp.swapaxes(relations, 1, 2)
    sent, object_own = call(
        pack_subject,
        "pack_subject",
        (shape((obj, strips + 8, LANES)), shape(object_factors.shape)),
        subject_factors,
        turned,
        object_factors,
        scratch=[
            pltpu.VMEM(subject_factors.shape, BF16),
            pltpu.VMEM(turned.shape, BF16),
            pltpu.SemaphoreType.DMA((3,)),
        ],
        spaces=[pltpu.HBM] * 3,
    )
    subject_all = lax.all_to_all(sent, "obj", 0, 0, tiled=True)
    stacked = (chips, object_part + count * rel_rows, width)
    sent = call(pack_object, "pack_object", shape(stacked), subject_all, object_own)
    own = lax.all_to_all(sent, "chip", 0, 0, tiled=True)
    other = to_other_core(own)
    square = (count, subjects, width)
    keep, send, carried, scores = call(
        grads,
        "grads",
        (shape(stacked), shape(stacked), shape(square), shape(labels.shape, F32)),
        subject_all,
        own,
        other,
        labels,
        scratch=[pltpu.VMEM(square, BF16), pltpu.VMEM(labels.shape, BF16)],
    )
    swapped = to_other_core(send)
    scale = float(count * objects * obj)
    packed = call(
        lambda *refs: subject_grads(*refs, total=scale),
        "subject_grads",
        shape((obj, strips + 8, LANES)),
        own,
        other,
        labels,
        scores,
        carried,
    )
    sent = call(
        add_pair,
        "add_pair",
        shape(stacked),
        keep,
        swapped,
        packed,
        spaces=[None, None, pl.ANY],
    )
    received = lax.all_to_all(sent, "chip", 0, 0, tiled=True)
    grad_object, sent = call(
        sum_object,
        "sum_object",
        (shape((object_part, width), F32), shape((obj, strips + 16, LANES))),
        received,
        packed,
    )
    received = lax.all_to_all(sent, "obj", 0, 0, tiled=True)
    scale = float(subjects * subj)
    grad_subject, grad_relations, loss = call(
        lambda *refs: sum_subject(*refs, total=scale),
        "sum_subject",
        (
            shape((subject_rows, width), F32),
            shape((count, rel_columns, rel_rows), F32),
            shape((1, subject_rows), F32),
        ),
        received,
    )
    return grad_subject, grad_object, jnp.swapaxes(grad_relations, 1, 2), loss.reshape(subject_rows)


def solution(mesh):
    subj, obj = mesh.shape["subj"], mesh.shape["obj"]
    cores = Mesh(mesh.devices.reshape(subj // 2, 2, obj), ("chip", "core", "obj"))
    rows = ("chip", "core")
    placed = (
        P((*rows, "obj"), None),
        P(("obj", *rows), None),
        P(None, rows, "obj"),
        P(None, rows, "obj"),
    )
    return jax.shard_map(
        body,
        mesh=cores,
        in_specs=placed,
        out_specs=(
            P((*rows, "obj"), None),
            P(("obj", *rows), None),
            P(None, rows, "obj"),
            P((*rows, "obj")),
        ),
        check_vma=False,
    )
```

```python
import jax
import jax.numpy as jnp
from jax import lax
from jax.experimental import pallas as pl
from jax.experimental.pallas import tpu as pltpu
from jax.sharding import Mesh
from jax.sharding import PartitionSpec as P

F32 = jnp.float32
BF16 = jnp.bfloat16
LANES = 128
CHUNK = 512
GRANT = 20 * 2**20


def halves_to_lanes(rows):
    return jnp.concatenate([rows[:, :8], rows[:, 8:]], axis=2)


def lanes_to_halves(tile):
    half = tile.shape[2] // 2
    return jnp.concatenate([tile[:, :, :half], tile[:, :, half:]], axis=1)


def columns_to_rows(block):
    return jnp.concatenate(
        [block[:, c : c + LANES] for c in range(0, block.shape[1], LANES)], axis=0
    )


def dot(a, b, contract):
    return lax.dot_general(a, b, ((contract[:1], contract[1:]), ((), ())), preferred_element_type=F32)


def pack_subject(
    subject_hbm, relation_hbm, object_hbm, out_ref, object_ref, subject_ref, relation_ref, arrived
):
    copies, _, _ = out_ref.shape
    loads = [
        pltpu.make_async_copy(subject_hbm, subject_ref, arrived.at[0]),
        pltpu.make_async_copy(relation_hbm, relation_ref, arrived.at[1]),
        pltpu.make_async_copy(object_hbm, object_ref, arrived.at[2]),
    ]
    for load in loads:
        load.start()
    for load in loads:
        load.wait()
    turned = jnp.concatenate([relation_ref[0], relation_ref[1]], axis=1).astype(F32)
    tile = halves_to_lanes(turned[None])[0].astype(BF16)
    factors = columns_to_rows(subject_ref[...])
    split = factors.shape[0]
    for p in range(copies):
        out_ref[p, :split] = factors
        out_ref[p, split:] = tile


def pack_object(gathered_ref, object_ref, out_ref):
    copies, _, width = out_ref.shape
    rows = object_ref.shape[0]
    split = gathered_ref.shape[1] - 8
    tiles = gathered_ref[:, split:, :].astype(F32)
    turned = lanes_to_halves(tiles)
    rel = turned.reshape(width, turned.shape[2]).T.astype(BF16)
    own = object_ref[...]
    for p in range(copies):
        out_ref[p, :rows] = own
        out_ref[p, rows:] = rel


def read_codes(labels_ref, _, sign_ref):
    for k in range(labels_ref.shape[0]):
        codes = labels_ref[k]
        sign_ref[k] = jnp.where(codes == 2, -1.0, jnp.where(codes > 0, 1.0, 0.0))


def stacked_rows(own_ref, other_ref, part, rows):
    first = lax.axis_index("core") == 0
    own = own_ref[:, rows * part : rows * (part + 1), :]
    other = other_ref[:, rows * part : rows * (part + 1), :]
    even = jnp.where(first, own, other)
    odd = jnp.where(first, other, own)
    return jnp.stack([even, odd], axis=1).reshape(-1, own.shape[2])


def store_owners(keep_ref, send_ref, part, rows, values):
    first = lax.axis_index("core") == 0
    by_core = values.astype(BF16).reshape(keep_ref.shape[0], 2, rows, values.shape[1])
    even, odd = by_core[:, 0], by_core[:, 1]
    span = slice(rows * part, rows * (part + 1))
    keep_ref[:, span, :] = jnp.where(first, even, odd)
    send_ref[:, span, :] = jnp.where(first, odd, even)


def grads(
    subject_ref,
    own_ref,
    other_ref,
    sign_ref,
    keep_ref,
    send_ref,
    carried_ref,
    signed_ref,
    left_ref,
    residual_ref,
):
    relations, size, _ = sign_ref.shape
    rows = size // (2 * keep_ref.shape[0])
    owners = subject_ref.shape[0]
    per_owner = size // owners
    subject = jnp.concatenate(
        [
            subject_ref[:, c * per_owner : (c + 1) * per_owner, :].reshape(size, LANES)
            for c in range(size // LANES)
        ],
        axis=1,
    )
    objects = stacked_rows(own_ref, other_ref, 0, rows)
    rels = [stacked_rows(own_ref, other_ref, k + 1, rows) for k in range(relations)]
    spans = [pl.ds(at, CHUNK) for at in range(0, size, CHUNK)]

    def project(k, span):
        left_ref[k, span] = dot(subject[span.start : span.start + CHUNK], rels[k], (1, 0)).astype(BF16)

    def settle(k, span):
        sign = sign_ref[k, span]
        signed = dot(left_ref[k, span], objects, (1, 1)) * sign
        signed_ref[k, span] = signed
        small = jnp.exp(-jnp.abs(signed))
        sigmoid = jnp.where(signed >= 0.0, 1.0, small) / (1.0 + small)
        residual_ref[k, span] = (sigmoid * sign).astype(BF16)

    def carry(k, span):
        carried_ref[k, span] = dot(residual_ref[k, span], objects, (1, 0)).astype(BF16)

    for k in range(relations):
        for step in (project, settle, carry):
            for span in spans:
                step(k, span)
    for k in range(relations):
        store_owners(keep_ref, send_ref, k + 1, rows, dot(subject, carried_ref[k], (0, 0)))
    grad_object = dot(residual_ref[0], left_ref[0], (0, 0))
    for k in range(1, relations):
        grad_object = grad_object + dot(residual_ref[k], left_ref[k], (0, 0))
    store_owners(keep_ref, send_ref, 0, rows, grad_object)


def add_pair(keep_ref, received_ref, _, out_ref):
    out_ref[...] = (keep_ref[...].astype(F32) + received_ref[...].astype(F32)).astype(BF16)


def subject_grads(
    own_ref, other_ref, signed_ref, sign_ref, carried_ref, out_ref, *, total
):
    relations, size, _ = signed_ref.shape
    rows = size // (2 * own_ref.shape[0])
    owners = out_ref.shape[0]
    per_owner = size // owners
    rels = [stacked_rows(own_ref, other_ref, k + 1, rows) for k in range(relations)]
    here = CHUNK // per_owner
    for at in range(0, size, CHUNK):
        span = pl.ds(at, CHUNK)
        loss = jnp.zeros((CHUNK, 1), F32)
        grad = jnp.zeros((CHUNK, size), F32)
        for k in range(relations):
            signed = signed_ref[k, span]
            cell = jnp.maximum(signed, 0.0) + jnp.log1p(jnp.exp(-jnp.abs(signed)))
            counted = sign_ref[k, span] != 0.0
            loss = loss + jnp.sum(jnp.where(counted, cell, 0.0), axis=1, keepdims=True)
            grad = grad + dot(carried_ref[k, span], rels[k], (1, 1))
        first = at // per_owner
        grad = grad.astype(BF16).reshape(here, per_owner, size)
        for c in range(size // LANES):
            out_ref[first : first + here, c * per_owner : (c + 1) * per_owner, :] = grad[
                :, :, c * LANES : (c + 1) * LANES
            ]
        part = jnp.broadcast_to(loss / total, (CHUNK, LANES // 2)).reshape(here, per_owner, -1)
        split = size // LANES * per_owner
        out_ref[first : first + here, split : split + 8, :] = halves_to_lanes(part).astype(BF16)


def sum_object(partial_ref, subject_ref, grad_ref, out_ref):
    rows = grad_ref.shape[0]
    width = grad_ref.shape[1]
    total = jnp.sum(partial_ref[...].astype(F32), axis=0)
    grad_ref[...] = total[:rows]
    turned = total[rows:].T
    owners = subject_ref.shape[0]
    tiles = halves_to_lanes(turned.reshape(owners, width // owners, -1)).astype(BF16)
    split = subject_ref.shape[1]
    out_ref[:, :split, :] = subject_ref[...]
    out_ref[:, split:, :] = tiles


def sum_subject(partial_ref, grad_ref, relation_ref, loss_ref, *, total):
    rows, width = grad_ref.shape
    summed = jnp.sum(partial_ref[...].astype(F32), axis=0)
    blocks = width // LANES
    grad_ref[...] = jnp.concatenate(
        [summed[c * rows : (c + 1) * rows] for c in range(blocks)], axis=1
    )
    at = blocks * rows
    loss = lanes_to_halves(summed[None, at : at + 8])[0]
    loss_ref[...] = loss.T[:1]
    turned = lanes_to_halves(summed[None, at + 8 : at + 16])[0] * (1.0 / total)
    columns = relation_ref.shape[2]
    for k in range(relation_ref.shape[0]):
        relation_ref[k] = turned[:, k * columns : (k + 1) * columns]


def shape(dims, dtype=BF16):
    return jax.ShapeDtypeStruct(dims, dtype)


def call(kernel, name, outs, *args, scratch=(), spaces=None):
    spaces = spaces or [None] * len(args)
    args = [
        pltpu.with_memory_space_constraint(a, s) if s is pltpu.HBM else a
        for a, s in zip(args, spaces)
    ]
    return pl.pallas_call(
        kernel,
        out_shape=outs,
        in_specs=[pl.BlockSpec(memory_space=space) for space in spaces],
        scratch_shapes=scratch,
        name=name,
        compiler_params=pltpu.CompilerParams(vmem_limit_bytes=GRANT),
    )(*args)


def to_other_core(array):
    return lax.ppermute(array, "core", [(0, 1), (1, 0)])


def body(subject_factors, object_factors, relations, labels):
    chips, obj = lax.axis_size("chip"), lax.axis_size("obj")
    subj = 2 * chips
    subject_rows, width = subject_factors.shape
    object_part = object_factors.shape[0]
    count, rel_rows, rel_columns = relations.shape
    _, subjects, objects = labels.shape
    strips = width // LANES * subject_rows
    turned = jnp.swapaxes(relations, 1, 2)
    sent, object_own = call(
        pack_subject,
        "pack_subject",
        (shape((obj, strips + 8, LANES)), shape(object_factors.shape)),
        subject_factors,
        turned,
        object_factors,
        scratch=[
            pltpu.VMEM(subject_factors.shape, BF16),
            pltpu.VMEM(turned.shape, BF16),
            pltpu.SemaphoreType.DMA((3,)),
        ],
        spaces=[pltpu.HBM] * 3,
    )
    subject_all = lax.all_to_all(sent, "obj", 0, 0, tiled=True)
    stacked = (chips, object_part + count * rel_rows, width)
    sent = call(pack_object, "pack_object", shape(stacked), subject_all, object_own)
    own = lax.all_to_all(sent, "chip", 0, 0, tiled=True)
    other = to_other_core(own)
    sign = call(
        read_codes, "read_codes", shape(labels.shape, F32), labels, own, spaces=[None, pl.ANY]
    )
    square = (count, subjects, width)
    keep, send, carried, signed = call(
        grads,
        "grads",
        (shape(stacked), shape(stacked), shape(square), shape(labels.shape, F32)),
        subject_all,
        own,
        other,
        sign,
        scratch=[pltpu.VMEM(square, BF16), pltpu.VMEM(labels.shape, BF16)],
    )
    swapped = to_other_core(send)
    scale = float(count * objects * obj)
    packed = call(
        lambda *refs: subject_grads(*refs, total=scale),
        "subject_grads",
        shape((obj, strips + 8, LANES)),
        own,
        other,
        signed,
        sign,
        carried,
    )
    sent = call(
        add_pair,
        "add_pair",
        shape(stacked),
        keep,
        swapped,
        packed,
        spaces=[None, None, pl.ANY],
    )
    received = lax.all_to_all(sent, "chip", 0, 0, tiled=True)
    grad_object, sent = call(
        sum_object,
        "sum_object",
        (shape((object_part, width), F32), shape((obj, strips + 16, LANES))),
        received,
        packed,
    )
    received = lax.all_to_all(sent, "obj", 0, 0, tiled=True)
    scale = float(subjects * subj)
    grad_subject, grad_relations, loss = call(
        lambda *refs: sum_subject(*refs, total=scale),
        "sum_subject",
        (
            shape((subject_rows, width), F32),
            shape((count, rel_columns, rel_rows), F32),
            shape((1, subject_rows), F32),
        ),
        received,
    )
    return grad_subject, grad_object, jnp.swapaxes(grad_relations, 1, 2), loss.reshape(subject_rows)


def solution(mesh):
    subj, obj = mesh.shape["subj"], mesh.shape["obj"]
    cores = Mesh(mesh.devices.reshape(subj // 2, 2, obj), ("chip", "core", "obj"))
    rows = ("chip", "core")
    placed = (
        P((*rows, "obj"), None),
        P(("obj", *rows), None),
        P(None, rows, "obj"),
        P(None, rows, "obj"),
    )
    return jax.shard_map(
        body,
        mesh=cores,
        in_specs=placed,
        out_specs=(
            P((*rows, "obj"), None),
            P(("obj", *rows), None),
            P(None, rows, "obj"),
            P((*rows, "obj")),
        ),
        check_vma=False,
    )
```

```python
import jax
import jax.numpy as jnp
from jax import lax
from jax.experimental import pallas as pl
from jax.experimental.pallas import tpu as pltpu
from jax.sharding import Mesh
from jax.sharding import PartitionSpec as P

F32 = jnp.float32
BF16 = jnp.bfloat16
LANES = 128
CHUNK = 512
GRANT = 20 * 2**20
PAIR = 2


def halves_to_lanes(rows):
    return jnp.concatenate([rows[:, :8], rows[:, 8:]], axis=2)


def lanes_to_halves(tile):
    half = tile.shape[2] // 2
    return jnp.concatenate([tile[:, :, :half], tile[:, :, half:]], axis=1)


def columns_to_rows(block):
    return jnp.concatenate(
        [block[:, c : c + LANES] for c in range(0, block.shape[1], LANES)], axis=0
    )


def dot(a, b, contract):
    return lax.dot_general(a, b, ((contract[:1], contract[1:]), ((), ())), preferred_element_type=F32)


def pack_subject(
    subject_hbm, relation_hbm, object_hbm, out_ref, object_ref, subject_ref, relation_ref, arrived
):
    copies, _, _ = out_ref.shape
    loads = [
        pltpu.make_async_copy(subject_hbm, subject_ref, arrived.at[0]),
        pltpu.make_async_copy(relation_hbm, relation_ref, arrived.at[1]),
        pltpu.make_async_copy(object_hbm, object_ref, arrived.at[2]),
    ]
    for load in loads:
        load.start()
    for load in loads:
        load.wait()
    turned = jnp.concatenate([relation_ref[0], relation_ref[1]], axis=1).astype(F32)
    tile = halves_to_lanes(turned[None])[0].astype(BF16)
    factors = columns_to_rows(subject_ref[...])
    split = factors.shape[0]
    for p in range(copies):
        out_ref[p, :split] = factors
        out_ref[p, split:] = tile


def pack_object(gathered_ref, object_ref, out_ref):
    copies, _, width = out_ref.shape
    rows = object_ref.shape[0]
    split = gathered_ref.shape[1] - 8
    tiles = gathered_ref[:, split:, :].astype(F32)
    turned = lanes_to_halves(tiles)
    rel = turned.reshape(width, turned.shape[2]).T.astype(BF16)
    own = object_ref[...]
    for p in range(copies):
        out_ref[p, :rows] = own
        out_ref[p, rows:] = rel


def read_codes(labels_ref, _, sign_ref):
    for k in range(labels_ref.shape[0]):
        codes = labels_ref[k]
        sign_ref[k] = jnp.where(codes == 2, -1.0, jnp.where(codes > 0, 1.0, 0.0))


def stacked_rows(own_ref, other_ref, part, rows):
    first = lax.axis_index("core") == 0
    own = own_ref[:, rows * part : rows * (part + 1), :]
    other = other_ref[:, rows * part : rows * (part + 1), :]
    even = jnp.where(first, own, other)
    odd = jnp.where(first, other, own)
    return jnp.stack([even, odd], axis=1).reshape(-1, own.shape[2])


def store_owners(keep_ref, send_ref, part, rows, values):
    first = lax.axis_index("core") == 0
    by_core = values.astype(BF16).reshape(keep_ref.shape[0], 2, rows, values.shape[1])
    even, odd = by_core[:, 0], by_core[:, 1]
    span = slice(rows * part, rows * (part + 1))
    keep_ref[:, span, :] = jnp.where(first, even, odd)
    send_ref[:, span, :] = jnp.where(first, odd, even)


def grads(
    subject_ref,
    own_ref,
    other_ref,
    sign_ref,
    keep_ref,
    send_ref,
    carried_ref,
    signed_ref,
    left_ref,
    residual_ref,
):
    relations, size, _ = sign_ref.shape
    rows = size // (2 * keep_ref.shape[0])
    owners = subject_ref.shape[0]
    per_owner = size // owners
    subject = jnp.concatenate(
        [
            subject_ref[:, c * per_owner : (c + 1) * per_owner, :].reshape(size, LANES)
            for c in range(size // LANES)
        ],
        axis=1,
    )
    objects = stacked_rows(own_ref, other_ref, 0, rows)
    rels = [stacked_rows(own_ref, other_ref, k + 1, rows) for k in range(relations)]
    spans = [pl.ds(at, CHUNK) for at in range(0, size, CHUNK)]

    def project(k, span):
        left_ref[k, span] = dot(subject[span.start : span.start + CHUNK], rels[k], (1, 0)).astype(BF16)

    def settle(k, span):
        sign = sign_ref[k, span]
        signed = dot(left_ref[k, span], objects, (1, 1)) * sign
        signed_ref[k, span] = signed
        small = jnp.exp(-jnp.abs(signed))
        sigmoid = jnp.where(signed >= 0.0, 1.0, small) / (1.0 + small)
        residual_ref[k, span] = (sigmoid * sign).astype(BF16)

    def carry(k, span):
        carried_ref[k, span] = dot(residual_ref[k, span], objects, (1, 0)).astype(BF16)

    for k in range(relations):
        for step in (project, settle, carry):
            for span in spans:
                step(k, span)
    for k in range(relations):
        store_owners(keep_ref, send_ref, k + 1, rows, dot(subject, carried_ref[k], (0, 0)))
    grad_object = dot(residual_ref[0], left_ref[0], (0, 0))
    for k in range(1, relations):
        grad_object = grad_object + dot(residual_ref[k], left_ref[k], (0, 0))
    store_owners(keep_ref, send_ref, 0, rows, grad_object)


def add_pair(keep_ref, received_ref, _, out_ref):
    out_ref[...] = (keep_ref[...].astype(F32) + received_ref[...].astype(F32)).astype(BF16)


def subject_grads(
    own_ref, other_ref, signed_ref, sign_ref, carried_ref, out_ref, loss_ref, *, total
):
    relations, size, _ = signed_ref.shape
    rows = size // (2 * own_ref.shape[0])
    owners = out_ref.shape[0]
    per_owner = size // owners
    rels = [stacked_rows(own_ref, other_ref, k + 1, rows) for k in range(relations)]
    here = CHUNK // per_owner
    for at in range(0, size, CHUNK):
        span = pl.ds(at, CHUNK)
        loss = jnp.zeros((CHUNK, 1), F32)
        grad = jnp.zeros((CHUNK, size), F32)
        for k in range(relations):
            signed = signed_ref[k, span]
            cell = jnp.maximum(signed, 0.0) + jnp.log1p(jnp.exp(-jnp.abs(signed)))
            counted = sign_ref[k, span] != 0.0
            loss = loss + jnp.sum(jnp.where(counted, cell, 0.0), axis=1, keepdims=True)
            grad = grad + dot(carried_ref[k, span], rels[k], (1, 1))
        first = at // per_owner
        grad = grad.astype(BF16).reshape(here, per_owner, size)
        for c in range(size // LANES):
            out_ref[first : first + here, c * per_owner : (c + 1) * per_owner, :] = grad[
                :, :, c * LANES : (c + 1) * LANES
            ]
        part = jnp.broadcast_to(loss / total, (CHUNK, LANES)).reshape(here, per_owner, LANES)
        entry = lax.broadcasted_iota(jnp.int32, part.shape, 1)
        lane = lax.broadcasted_iota(jnp.int32, part.shape, 2)
        loss_ref[first : first + here] = jnp.sum(jnp.where(entry == lane, part, 0.0), axis=1)


def sum_relations(partial_ref, subject_ref, loss_ref, out_ref, *, rows):
    width = partial_ref.shape[2]
    total = jnp.sum(partial_ref[:, rows:, :].astype(F32), axis=0)
    turned = total.T
    owners, strips, _ = subject_ref.shape
    tiles = halves_to_lanes(turned.reshape(owners, width // owners, -1)).astype(BF16)
    piece = strips + 8 + PAIR
    for p in range(owners):
        at = p * piece
        out_ref[at : at + strips] = subject_ref[p]
        out_ref[at + strips : at + strips + 8] = tiles[p]
        row = jnp.broadcast_to(loss_ref[p : p + 1], (PAIR, LANES))
        out_ref[at + strips + 8 : at + piece] = row.astype(BF16)


def sum_factors(
    partial_ref, object_ref, grad_ref, grad_object_ref, relation_ref, loss_ref, *, owners, total
):
    rows, width = grad_ref.shape
    grad_object_ref[...] = jnp.sum(
        object_ref[:, : grad_object_ref.shape[0], :].astype(F32), axis=0
    )
    piece = partial_ref.shape[0] // owners
    summed = partial_ref[:piece].astype(F32)
    for p in range(1, owners):
        summed = summed + partial_ref[p * piece : (p + 1) * piece].astype(F32)
    blocks = width // LANES
    grad_ref[...] = jnp.concatenate(
        [summed[c * rows : (c + 1) * rows] for c in range(blocks)], axis=1
    )
    at = blocks * rows
    turned = lanes_to_halves(summed[None, at : at + 8])[0] * (1.0 / total)
    columns = relation_ref.shape[2]
    for k in range(relation_ref.shape[0]):
        relation_ref[k] = turned[:, k * columns : (k + 1) * columns]
    loss_ref[...] = summed[at + 8 : at + 9, :rows]


def shape(dims, dtype=BF16):
    return jax.ShapeDtypeStruct(dims, dtype)


def call(kernel, name, outs, *args, scratch=(), spaces=None):
    spaces = spaces or [None] * len(args)
    args = [
        pltpu.with_memory_space_constraint(a, s) if s is pltpu.HBM else a
        for a, s in zip(args, spaces)
    ]
    return pl.pallas_call(
        kernel,
        out_shape=outs,
        in_specs=[pl.BlockSpec(memory_space=space) for space in spaces],
        scratch_shapes=scratch,
        name=name,
        compiler_params=pltpu.CompilerParams(vmem_limit_bytes=GRANT),
    )(*args)


def to_other_core(array):
    return lax.ppermute(array, "core", [(0, 1), (1, 0)])


def body(subject_factors, object_factors, relations, labels):
    chips, obj = lax.axis_size("chip"), lax.axis_size("obj")
    subj = 2 * chips
    subject_rows, width = subject_factors.shape
    object_part = object_factors.shape[0]
    count, rel_rows, rel_columns = relations.shape
    _, subjects, objects = labels.shape
    strips = width // LANES * subject_rows
    turned = jnp.swapaxes(relations, 1, 2)
    sent, object_own = call(
        pack_subject,
        "pack_subject",
        (shape((obj, strips + 8, LANES)), shape(object_factors.shape)),
        subject_factors,
        turned,
        object_factors,
        scratch=[
            pltpu.VMEM(subject_factors.shape, BF16),
            pltpu.VMEM(turned.shape, BF16),
            pltpu.SemaphoreType.DMA((3,)),
        ],
        spaces=[pltpu.HBM] * 3,
    )
    subject_all = lax.all_to_all(sent, "obj", 0, 0, tiled=True)
    stacked = (chips, object_part + count * rel_rows, width)
    sent = call(pack_object, "pack_object", shape(stacked), subject_all, object_own)
    own = lax.all_to_all(sent, "chip", 0, 0, tiled=True)
    other = to_other_core(own)
    sign = call(
        read_codes, "read_codes", shape(labels.shape, F32), labels, own, spaces=[None, pl.ANY]
    )
    square = (count, subjects, width)
    keep, send, carried, signed = call(
        grads,
        "grads",
        (shape(stacked), shape(stacked), shape(square), shape(labels.shape, F32)),
        subject_all,
        own,
        other,
        sign,
        scratch=[pltpu.VMEM(square, BF16), pltpu.VMEM(labels.shape, BF16)],
    )
    swapped = to_other_core(send)
    scale = float(count * objects * obj)
    packed, loss_rows = call(
        lambda *refs: subject_grads(*refs, total=scale),
        "subject_grads",
        (shape((obj, strips, LANES)), shape((obj, LANES), F32)),
        own,
        other,
        signed,
        sign,
        carried,
    )
    sent = call(
        add_pair,
        "add_pair",
        shape(stacked),
        keep,
        swapped,
        packed,
        spaces=[None, None, pl.ANY],
    )
    object_partial = lax.all_to_all(sent, "chip", 0, 0, tiled=True)
    piece = strips + 8 + PAIR
    sent = call(
        lambda *refs: sum_relations(*refs, rows=object_part),
        "sum_relations",
        shape((obj * piece, LANES)),
        object_partial,
        packed,
        loss_rows,
    )
    sent = sent.reshape(-1, PAIR, LANES)
    received = lax.all_to_all(sent, "obj", 0, 0, tiled=True).reshape(-1, LANES)
    scale = float(subjects * subj)
    grad_subject, grad_object, grad_relations, loss = call(
        lambda *refs: sum_factors(*refs, owners=obj, total=scale),
        "sum_factors",
        (
            shape((subject_rows, width), F32),
            shape((object_part, width), F32),
            shape((count, rel_columns, rel_rows), F32),
            shape((1, subject_rows), F32),
        ),
        received,
        object_partial,
    )
    return grad_subject, grad_object, jnp.swapaxes(grad_relations, 1, 2), loss.reshape(subject_rows)


def solution(mesh):
    subj, obj = mesh.shape["subj"], mesh.shape["obj"]
    cores = Mesh(mesh.devices.reshape(subj // 2, 2, obj), ("chip", "core", "obj"))
    rows = ("chip", "core")
    placed = (
        P((*rows, "obj"), None),
        P(("obj", *rows), None),
        P(None, rows, "obj"),
        P(None, rows, "obj"),
    )
    return jax.shard_map(
        body,
        mesh=cores,
        in_specs=placed,
        out_specs=(
            P((*rows, "obj"), None),
            P(("obj", *rows), None),
            P(None, rows, "obj"),
            P((*rows, "obj")),
        ),
        check_vma=False,
    )
```

```python
import jax
import jax.numpy as jnp
from jax import lax
from jax.experimental import pallas as pl
from jax.experimental.pallas import tpu as pltpu
from jax.sharding import Mesh
from jax.sharding import PartitionSpec as P

F32 = jnp.float32
BF16 = jnp.bfloat16
LANES = 128
CHUNK = 512
GRANT = 20 * 2**20
PAIR = 2


def halves_to_lanes(rows):
    return jnp.concatenate([rows[:, :8], rows[:, 8:]], axis=2)


def lanes_to_halves(tile):
    half = tile.shape[2] // 2
    return jnp.concatenate([tile[:, :, :half], tile[:, :, half:]], axis=1)


def columns_to_rows(block):
    return jnp.concatenate(
        [block[:, c : c + LANES] for c in range(0, block.shape[1], LANES)], axis=0
    )


def dot(a, b, contract):
    return lax.dot_general(a, b, ((contract[:1], contract[1:]), ((), ())), preferred_element_type=F32)


def pack_subject(
    subject_hbm, relation_hbm, object_hbm, out_ref, object_ref, subject_ref, relation_ref, arrived
):
    copies, _, _ = out_ref.shape
    loads = [
        pltpu.make_async_copy(subject_hbm, subject_ref, arrived.at[0]),
        pltpu.make_async_copy(relation_hbm, relation_ref, arrived.at[1]),
        pltpu.make_async_copy(object_hbm, object_ref, arrived.at[2]),
    ]
    for load in loads:
        load.start()
    for load in loads:
        load.wait()
    turned = jnp.concatenate([relation_ref[0], relation_ref[1]], axis=1).astype(F32)
    tile = halves_to_lanes(turned[None])[0].astype(BF16)
    factors = columns_to_rows(subject_ref[...])
    split = factors.shape[0]
    for p in range(copies):
        out_ref[p, :split] = factors
        out_ref[p, split:] = tile


def pack_object(gathered_ref, object_ref, out_ref):
    copies, _, width = out_ref.shape
    rows = object_ref.shape[0]
    split = gathered_ref.shape[1] - 8
    tiles = gathered_ref[:, split:, :].astype(F32)
    turned = lanes_to_halves(tiles)
    rel = turned.reshape(width, turned.shape[2]).T.astype(BF16)
    own = object_ref[...]
    for p in range(copies):
        out_ref[p, :rows] = own
        out_ref[p, rows:] = rel


def read_codes(labels_ref, _, sign_ref):
    for k in range(labels_ref.shape[0]):
        codes = labels_ref[k]
        sign_ref[k] = jnp.where(codes == 2, -1.0, jnp.where(codes > 0, 1.0, 0.0))


def stacked_rows(own_ref, other_ref, part, rows):
    first = lax.axis_index("core") == 0
    own = own_ref[:, rows * part : rows * (part + 1), :]
    other = other_ref[:, rows * part : rows * (part + 1), :]
    even = jnp.where(first, own, other)
    odd = jnp.where(first, other, own)
    return jnp.stack([even, odd], axis=1).reshape(-1, own.shape[2])


def store_owners(keep_ref, send_ref, part, rows, values):
    first = lax.axis_index("core") == 0
    by_core = values.astype(BF16).reshape(keep_ref.shape[0], 2, rows, values.shape[1])
    even, odd = by_core[:, 0], by_core[:, 1]
    span = slice(rows * part, rows * (part + 1))
    keep_ref[:, span, :] = jnp.where(first, even, odd)
    send_ref[:, span, :] = jnp.where(first, odd, even)


def grads(
    subject_ref,
    own_ref,
    other_ref,
    sign_ref,
    keep_ref,
    send_ref,
    carried_ref,
    signed_ref,
    left_ref,
    residual_ref,
):
    relations, size, _ = sign_ref.shape
    rows = size // (2 * keep_ref.shape[0])
    owners = subject_ref.shape[0]
    per_owner = size // owners
    subject = jnp.concatenate(
        [
            subject_ref[:, c * per_owner : (c + 1) * per_owner, :].reshape(size, LANES)
            for c in range(size // LANES)
        ],
        axis=1,
    )
    objects = stacked_rows(own_ref, other_ref, 0, rows)
    rels = [stacked_rows(own_ref, other_ref, k + 1, rows) for k in range(relations)]

    def project(k):
        left_ref[k] = dot(subject, rels[k], (1, 0)).astype(BF16)

    def score(k):
        signed_ref[k] = dot(left_ref[k], objects, (1, 1))

    def settle(k):
        sign = sign_ref[k]
        signed = signed_ref[k] * sign
        small = jnp.exp(-jnp.abs(signed))
        sigmoid = jnp.where(signed >= 0.0, 1.0, small) / (1.0 + small)
        residual_ref[k] = (sigmoid * sign).astype(BF16)

    def carry(k):
        carried_ref[k] = dot(residual_ref[k], objects, (1, 0)).astype(BF16)

    def relation_grad(k):
        store_owners(keep_ref, send_ref, k + 1, rows, dot(subject, carried_ref[k], (0, 0)))

    for k in range(relations):
        project(k)
        score(k)
        settle(k)
        if k > 0:
            relation_grad(k - 1)
        carry(k)
    relation_grad(relations - 1)
    grad_object = dot(residual_ref[0], left_ref[0], (0, 0))
    for k in range(1, relations):
        grad_object = grad_object + dot(residual_ref[k], left_ref[k], (0, 0))
    store_owners(keep_ref, send_ref, 0, rows, grad_object)


def add_pair(keep_ref, received_ref, _, out_ref):
    out_ref[...] = (keep_ref[...].astype(F32) + received_ref[...].astype(F32)).astype(BF16)


def subject_grads(
    own_ref, other_ref, signed_ref, sign_ref, carried_ref, out_ref, loss_ref, *, total
):
    relations, size, _ = signed_ref.shape
    rows = size // (2 * own_ref.shape[0])
    owners = out_ref.shape[0]
    per_owner = size // owners
    rels = [stacked_rows(own_ref, other_ref, k + 1, rows) for k in range(relations)]
    here = CHUNK // per_owner
    for at in range(0, size, CHUNK):
        span = pl.ds(at, CHUNK)
        loss = jnp.zeros((CHUNK, 1), F32)
        grad = jnp.zeros((CHUNK, size), F32)
        for k in range(relations):
            sign = sign_ref[k, span]
            signed = signed_ref[k, span] * sign
            cell = jnp.maximum(signed, 0.0) + jnp.log1p(jnp.exp(-jnp.abs(signed)))
            counted = sign != 0.0
            loss = loss + jnp.sum(jnp.where(counted, cell, 0.0), axis=1, keepdims=True)
            grad = grad + dot(carried_ref[k, span], rels[k], (1, 1))
        first = at // per_owner
        grad = grad.astype(BF16).reshape(here, per_owner, size)
        for c in range(size // LANES):
            out_ref[first : first + here, c * per_owner : (c + 1) * per_owner, :] = grad[
                :, :, c * LANES : (c + 1) * LANES
            ]
        part = jnp.broadcast_to(loss / total, (CHUNK, LANES)).reshape(here, per_owner, LANES)
        entry = lax.broadcasted_iota(jnp.int32, part.shape, 1)
        lane = lax.broadcasted_iota(jnp.int32, part.shape, 2)
        loss_ref[first : first + here] = jnp.sum(jnp.where(entry == lane, part, 0.0), axis=1)


def sum_relations(partial_ref, subject_ref, loss_ref, out_ref, *, rows):
    width = partial_ref.shape[2]
    total = jnp.sum(partial_ref[:, rows:, :].astype(F32), axis=0)
    turned = total.T
    owners, strips, _ = subject_ref.shape
    tiles = halves_to_lanes(turned.reshape(owners, width // owners, -1)).astype(BF16)
    piece = strips + 8 + PAIR
    for p in range(owners):
        at = p * piece
        out_ref[at : at + strips] = subject_ref[p]
        out_ref[at + strips : at + strips + 8] = tiles[p]
        row = jnp.broadcast_to(loss_ref[p : p + 1], (PAIR, LANES))
        out_ref[at + strips + 8 : at + piece] = row.astype(BF16)


def sum_factors(
    partial_ref, object_ref, grad_ref, grad_object_ref, relation_ref, loss_ref, *, owners, total
):
    rows, width = grad_ref.shape
    grad_object_ref[...] = jnp.sum(
        object_ref[:, : grad_object_ref.shape[0], :].astype(F32), axis=0
    )
    piece = partial_ref.shape[0] // owners
    summed = partial_ref[:piece].astype(F32)
    for p in range(1, owners):
        summed = summed + partial_ref[p * piece : (p + 1) * piece].astype(F32)
    blocks = width // LANES
    grad_ref[...] = jnp.concatenate(
        [summed[c * rows : (c + 1) * rows] for c in range(blocks)], axis=1
    )
    at = blocks * rows
    turned = lanes_to_halves(summed[None, at : at + 8])[0] * (1.0 / total)
    columns = relation_ref.shape[2]
    for k in range(relation_ref.shape[0]):
        relation_ref[k] = turned[:, k * columns : (k + 1) * columns]
    loss_ref[...] = summed[at + 8 : at + 9, :rows]


def shape(dims, dtype=BF16):
    return jax.ShapeDtypeStruct(dims, dtype)


def call(kernel, name, outs, *args, scratch=(), spaces=None):
    spaces = spaces or [None] * len(args)
    args = [
        pltpu.with_memory_space_constraint(a, s) if s is pltpu.HBM else a
        for a, s in zip(args, spaces)
    ]
    return pl.pallas_call(
        kernel,
        out_shape=outs,
        in_specs=[pl.BlockSpec(memory_space=space) for space in spaces],
        scratch_shapes=scratch,
        name=name,
        compiler_params=pltpu.CompilerParams(vmem_limit_bytes=GRANT),
    )(*args)


def to_other_core(array):
    return lax.ppermute(array, "core", [(0, 1), (1, 0)])


def body(subject_factors, object_factors, relations, labels):
    chips, obj = lax.axis_size("chip"), lax.axis_size("obj")
    subj = 2 * chips
    subject_rows, width = subject_factors.shape
    object_part = object_factors.shape[0]
    count, rel_rows, rel_columns = relations.shape
    _, subjects, objects = labels.shape
    strips = width // LANES * subject_rows
    turned = jnp.swapaxes(relations, 1, 2)
    sent, object_own = call(
        pack_subject,
        "pack_subject",
        (shape((obj, strips + 8, LANES)), shape(object_factors.shape)),
        subject_factors,
        turned,
        object_factors,
        scratch=[
            pltpu.VMEM(subject_factors.shape, BF16),
            pltpu.VMEM(turned.shape, BF16),
            pltpu.SemaphoreType.DMA((3,)),
        ],
        spaces=[pltpu.HBM] * 3,
    )
    subject_all = lax.all_to_all(sent, "obj", 0, 0, tiled=True)
    stacked = (chips, object_part + count * rel_rows, width)
    sent = call(pack_object, "pack_object", shape(stacked), subject_all, object_own)
    own = lax.all_to_all(sent, "chip", 0, 0, tiled=True)
    other = to_other_core(own)
    sign = call(
        read_codes, "read_codes", shape(labels.shape, F32), labels, own, spaces=[None, pl.ANY]
    )
    square = (count, subjects, width)
    keep, send, carried, signed = call(
        grads,
        "grads",
        (shape(stacked), shape(stacked), shape(square), shape(labels.shape, F32)),
        subject_all,
        own,
        other,
        sign,
        scratch=[pltpu.VMEM(square, BF16), pltpu.VMEM(labels.shape, BF16)],
    )
    swapped = to_other_core(send)
    scale = float(count * objects * obj)
    packed, loss_rows = call(
        lambda *refs: subject_grads(*refs, total=scale),
        "subject_grads",
        (shape((obj, strips, LANES)), shape((obj, LANES), F32)),
        own,
        other,
        signed,
        sign,
        carried,
    )
    sent = call(
        add_pair,
        "add_pair",
        shape(stacked),
        keep,
        swapped,
        packed,
        spaces=[None, None, pl.ANY],
    )
    object_partial = lax.all_to_all(sent, "chip", 0, 0, tiled=True)
    piece = strips + 8 + PAIR
    sent = call(
        lambda *refs: sum_relations(*refs, rows=object_part),
        "sum_relations",
        shape((obj * piece, LANES)),
        object_partial,
        packed,
        loss_rows,
    )
    sent = sent.reshape(-1, PAIR, LANES)
    received = lax.all_to_all(sent, "obj", 0, 0, tiled=True).reshape(-1, LANES)
    scale = float(subjects * subj)
    grad_subject, grad_object, grad_relations, loss = call(
        lambda *refs: sum_factors(*refs, owners=obj, total=scale),
        "sum_factors",
        (
            shape((subject_rows, width), F32),
            shape((object_part, width), F32),
            shape((count, rel_columns, rel_rows), F32),
            shape((1, subject_rows), F32),
        ),
        received,
        object_partial,
    )
    return grad_subject, grad_object, jnp.swapaxes(grad_relations, 1, 2), loss.reshape(subject_rows)


def solution(mesh):
    subj, obj = mesh.shape["subj"], mesh.shape["obj"]
    cores = Mesh(mesh.devices.reshape(subj // 2, 2, obj), ("chip", "core", "obj"))
    rows = ("chip", "core")
    placed = (
        P((*rows, "obj"), None),
        P(("obj", *rows), None),
        P(None, rows, "obj"),
        P(None, rows, "obj"),
    )
    return jax.shard_map(
        body,
        mesh=cores,
        in_specs=placed,
        out_specs=(
            P((*rows, "obj"), None),
            P(("obj", *rows), None),
            P(None, rows, "obj"),
            P((*rows, "obj")),
        ),
        check_vma=False,
    )
```

```python
import jax
import jax.numpy as jnp
from jax import lax
from jax.experimental import pallas as pl
from jax.experimental.pallas import tpu as pltpu
from jax.sharding import Mesh
from jax.sharding import PartitionSpec as P

F32 = jnp.float32
BF16 = jnp.bfloat16
LANES = 128
CHUNK = 512
GRANT = 20 * 2**20
PAIR = 2


def halves_to_lanes(rows):
    return jnp.concatenate([rows[:, :8], rows[:, 8:]], axis=2)


def lanes_to_halves(tile):
    half = tile.shape[2] // 2
    return jnp.concatenate([tile[:, :, :half], tile[:, :, half:]], axis=1)


def columns_to_rows(block):
    return jnp.concatenate(
        [block[:, c : c + LANES] for c in range(0, block.shape[1], LANES)], axis=0
    )


def dot(a, b, contract):
    return lax.dot_general(a, b, ((contract[:1], contract[1:]), ((), ())), preferred_element_type=F32)


def pack_subject(
    subject_hbm, relation_hbm, object_hbm, out_ref, object_ref, subject_ref, relation_ref, arrived
):
    copies, _, _ = out_ref.shape
    loads = [
        pltpu.make_async_copy(subject_hbm, subject_ref, arrived.at[0]),
        pltpu.make_async_copy(relation_hbm, relation_ref, arrived.at[1]),
        pltpu.make_async_copy(object_hbm, object_ref, arrived.at[2]),
    ]
    for load in loads:
        load.start()
    for load in loads[:2]:
        load.wait()
    turned = jnp.concatenate([relation_ref[0], relation_ref[1]], axis=1).astype(F32)
    tile = halves_to_lanes(turned[None])[0].astype(BF16)
    factors = columns_to_rows(subject_ref[...])
    split = factors.shape[0]
    for p in range(copies):
        out_ref[p, :split] = factors
        out_ref[p, split:] = tile
    loads[2].wait()


def pack_object(gathered_ref, object_ref, out_ref):
    copies, _, width = out_ref.shape
    rows = object_ref.shape[0]
    split = gathered_ref.shape[1] - 8
    tiles = gathered_ref[:, split:, :].astype(F32)
    turned = lanes_to_halves(tiles)
    rel = turned.reshape(width, turned.shape[2]).T.astype(BF16)
    own = object_ref[...]
    for p in range(copies):
        out_ref[p, :rows] = own
        out_ref[p, rows:] = rel


def read_codes(labels_hbm, _, sign_ref, labels_ref, arrived):
    relations = labels_ref.shape[0]
    loads = [
        pltpu.make_async_copy(labels_hbm.at[k], labels_ref.at[k], arrived.at[k])
        for k in range(relations)
    ]
    for load in loads:
        load.start()
    for k in range(relations):
        loads[k].wait()
        codes = labels_ref[k]
        sign_ref[k] = jnp.where(codes == 2, -1.0, jnp.where(codes > 0, 1.0, 0.0))


def stacked_rows(own_ref, other_ref, part, rows):
    first = lax.axis_index("core") == 0
    own = own_ref[:, rows * part : rows * (part + 1), :]
    other = other_ref[:, rows * part : rows * (part + 1), :]
    even = jnp.where(first, own, other)
    odd = jnp.where(first, other, own)
    return jnp.stack([even, odd], axis=1).reshape(-1, own.shape[2])


def store_owners(keep_ref, send_ref, part, rows, values):
    first = lax.axis_index("core") == 0
    by_core = values.astype(BF16).reshape(keep_ref.shape[0], 2, rows, values.shape[1])
    even, odd = by_core[:, 0], by_core[:, 1]
    span = slice(rows * part, rows * (part + 1))
    keep_ref[:, span, :] = jnp.where(first, even, odd)
    send_ref[:, span, :] = jnp.where(first, odd, even)


def grads(
    subject_ref,
    own_ref,
    other_ref,
    sign_ref,
    keep_ref,
    send_ref,
    carried_ref,
    signed_ref,
    left_ref,
    residual_ref,
):
    relations, size, _ = sign_ref.shape
    rows = size // (2 * keep_ref.shape[0])
    owners = subject_ref.shape[0]
    per_owner = size // owners
    subject = jnp.concatenate(
        [
            subject_ref[:, c * per_owner : (c + 1) * per_owner, :].reshape(size, LANES)
            for c in range(size // LANES)
        ],
        axis=1,
    )
    objects = stacked_rows(own_ref, other_ref, 0, rows)
    rels = [stacked_rows(own_ref, other_ref, k + 1, rows) for k in range(relations)]

    def project(k):
        left_ref[k] = dot(subject, rels[k], (1, 0)).astype(BF16)

    def score(k):
        signed_ref[k] = dot(left_ref[k], objects, (1, 1))

    def settle(k):
        sign = sign_ref[k]
        signed = signed_ref[k] * sign
        small = jnp.exp(-jnp.abs(signed))
        sigmoid = jnp.where(signed >= 0.0, 1.0, small) / (1.0 + small)
        residual_ref[k] = (sigmoid * sign).astype(BF16)

    def carry(k):
        carried_ref[k] = dot(residual_ref[k], objects, (1, 0)).astype(BF16)

    def relation_grad(k):
        store_owners(keep_ref, send_ref, k + 1, rows, dot(subject, carried_ref[k], (0, 0)))

    for k in range(relations):
        project(k)
        score(k)
        settle(k)
        if k > 0:
            relation_grad(k - 1)
        carry(k)
    relation_grad(relations - 1)
    grad_object = dot(residual_ref[0], left_ref[0], (0, 0))
    for k in range(1, relations):
        grad_object = grad_object + dot(residual_ref[k], left_ref[k], (0, 0))
    store_owners(keep_ref, send_ref, 0, rows, grad_object)


def add_pair(keep_ref, received_ref, _, out_ref):
    out_ref[...] = (keep_ref[...].astype(F32) + received_ref[...].astype(F32)).astype(BF16)


def subject_grads(
    own_ref, other_ref, signed_ref, sign_ref, carried_ref, out_ref, loss_ref, *, total
):
    relations, size, _ = signed_ref.shape
    rows = size // (2 * own_ref.shape[0])
    owners = out_ref.shape[0]
    per_owner = size // owners
    rels = [stacked_rows(own_ref, other_ref, k + 1, rows) for k in range(relations)]
    here = CHUNK // per_owner
    for at in range(0, size, CHUNK):
        span = pl.ds(at, CHUNK)
        loss = jnp.zeros((CHUNK, 1), F32)
        grad = jnp.zeros((CHUNK, size), F32)
        for k in range(relations):
            sign = sign_ref[k, span]
            signed = signed_ref[k, span] * sign
            cell = jnp.maximum(signed, 0.0) + jnp.log1p(jnp.exp(-jnp.abs(signed)))
            counted = sign != 0.0
            loss = loss + jnp.sum(jnp.where(counted, cell, 0.0), axis=1, keepdims=True)
            grad = grad + dot(carried_ref[k, span], rels[k], (1, 1))
        first = at // per_owner
        grad = grad.astype(BF16).reshape(here, per_owner, size)
        for c in range(size // LANES):
            out_ref[first : first + here, c * per_owner : (c + 1) * per_owner, :] = grad[
                :, :, c * LANES : (c + 1) * LANES
            ]
        part = jnp.broadcast_to(loss / total, (CHUNK, LANES)).reshape(here, per_owner, LANES)
        entry = lax.broadcasted_iota(jnp.int32, part.shape, 1)
        lane = lax.broadcasted_iota(jnp.int32, part.shape, 2)
        loss_ref[first : first + here] = jnp.sum(jnp.where(entry == lane, part, 0.0), axis=1)


def sum_relations(partial_ref, subject_ref, loss_ref, out_ref, *, rows):
    width = partial_ref.shape[2]
    total = jnp.sum(partial_ref[:, rows:, :].astype(F32), axis=0)
    turned = total.T
    owners, strips, _ = subject_ref.shape
    tiles = halves_to_lanes(turned.reshape(owners, width // owners, -1)).astype(BF16)
    piece = strips + 8 + PAIR
    for p in range(owners):
        at = p * piece
        out_ref[at : at + strips] = subject_ref[p]
        out_ref[at + strips : at + strips + 8] = tiles[p]
        row = jnp.broadcast_to(loss_ref[p : p + 1], (PAIR, LANES))
        out_ref[at + strips + 8 : at + piece] = row.astype(BF16)


def sum_factors(
    partial_ref, object_ref, grad_ref, grad_object_ref, relation_ref, loss_ref, *, owners, total
):
    rows, width = grad_ref.shape
    grad_object_ref[...] = jnp.sum(
        object_ref[:, : grad_object_ref.shape[0], :].astype(F32), axis=0
    )
    piece = partial_ref.shape[0] // owners
    summed = partial_ref[:piece].astype(F32)
    for p in range(1, owners):
        summed = summed + partial_ref[p * piece : (p + 1) * piece].astype(F32)
    blocks = width // LANES
    grad_ref[...] = jnp.concatenate(
        [summed[c * rows : (c + 1) * rows] for c in range(blocks)], axis=1
    )
    at = blocks * rows
    turned = lanes_to_halves(summed[None, at : at + 8])[0] * (1.0 / total)
    columns = relation_ref.shape[2]
    for k in range(relation_ref.shape[0]):
        relation_ref[k] = turned[:, k * columns : (k + 1) * columns]
    loss_ref[...] = summed[at + 8 : at + 9, :rows]


def shape(dims, dtype=BF16):
    return jax.ShapeDtypeStruct(dims, dtype)


def call(kernel, name, outs, *args, scratch=(), spaces=None):
    spaces = spaces or [None] * len(args)
    args = [
        pltpu.with_memory_space_constraint(a, s) if s is pltpu.HBM else a
        for a, s in zip(args, spaces)
    ]
    return pl.pallas_call(
        kernel,
        out_shape=outs,
        in_specs=[pl.BlockSpec(memory_space=space) for space in spaces],
        scratch_shapes=scratch,
        name=name,
        compiler_params=pltpu.CompilerParams(vmem_limit_bytes=GRANT),
    )(*args)


def to_other_core(array):
    return lax.ppermute(array, "core", [(0, 1), (1, 0)])


def body(subject_factors, object_factors, relations, labels):
    chips, obj = lax.axis_size("chip"), lax.axis_size("obj")
    subj = 2 * chips
    subject_rows, width = subject_factors.shape
    object_part = object_factors.shape[0]
    count, rel_rows, rel_columns = relations.shape
    _, subjects, objects = labels.shape
    strips = width // LANES * subject_rows
    turned = jnp.swapaxes(relations, 1, 2)
    sent, object_own = call(
        pack_subject,
        "pack_subject",
        (shape((obj, strips + 8, LANES)), shape(object_factors.shape)),
        subject_factors,
        turned,
        object_factors,
        scratch=[
            pltpu.VMEM(subject_factors.shape, BF16),
            pltpu.VMEM(turned.shape, BF16),
            pltpu.SemaphoreType.DMA((3,)),
        ],
        spaces=[pltpu.HBM] * 3,
    )
    subject_all = lax.all_to_all(sent, "obj", 0, 0, tiled=True)
    stacked = (chips, object_part + count * rel_rows, width)
    sent = call(pack_object, "pack_object", shape(stacked), subject_all, object_own)
    own = lax.all_to_all(sent, "chip", 0, 0, tiled=True)
    other = to_other_core(own)
    sign = call(
        read_codes,
        "read_codes",
        shape(labels.shape, F32),
        labels,
        own,
        scratch=[pltpu.VMEM(labels.shape, labels.dtype), pltpu.SemaphoreType.DMA((count,))],
        spaces=[pltpu.HBM, pl.ANY],
    )
    square = (count, subjects, width)
    keep, send, carried, signed = call(
        grads,
        "grads",
        (shape(stacked), shape(stacked), shape(square), shape(labels.shape, F32)),
        subject_all,
        own,
        other,
        sign,
        scratch=[pltpu.VMEM(square, BF16), pltpu.VMEM(labels.shape, BF16)],
    )
    swapped = to_other_core(send)
    scale = float(count * objects * obj)
    packed, loss_rows = call(
        lambda *refs: subject_grads(*refs, total=scale),
        "subject_grads",
        (shape((obj, strips, LANES)), shape((obj, LANES), F32)),
        own,
        other,
        signed,
        sign,
        carried,
    )
    sent = call(
        add_pair,
        "add_pair",
        shape(stacked),
        keep,
        swapped,
        packed,
        spaces=[None, None, pl.ANY],
    )
    object_partial = lax.all_to_all(sent, "chip", 0, 0, tiled=True)
    piece = strips + 8 + PAIR
    sent = call(
        lambda *refs: sum_relations(*refs, rows=object_part),
        "sum_relations",
        shape((obj * piece, LANES)),
        object_partial,
        packed,
        loss_rows,
    )
    sent = sent.reshape(-1, PAIR, LANES)
    received = lax.all_to_all(sent, "obj", 0, 0, tiled=True).reshape(-1, LANES)
    scale = float(subjects * subj)
    grad_subject, grad_object, grad_relations, loss = call(
        lambda *refs: sum_factors(*refs, owners=obj, total=scale),
        "sum_factors",
        (
            shape((subject_rows, width), F32),
            shape((object_part, width), F32),
            shape((count, rel_columns, rel_rows), F32),
            shape((1, subject_rows), F32),
        ),
        received,
        object_partial,
    )
    return grad_subject, grad_object, jnp.swapaxes(grad_relations, 1, 2), loss.reshape(subject_rows)


def solution(mesh):
    subj, obj = mesh.shape["subj"], mesh.shape["obj"]
    cores = Mesh(mesh.devices.reshape(subj // 2, 2, obj), ("chip", "core", "obj"))
    rows = ("chip", "core")
    placed = (
        P((*rows, "obj"), None),
        P(("obj", *rows), None),
        P(None, rows, "obj"),
        P(None, rows, "obj"),
    )
    return jax.shard_map(
        body,
        mesh=cores,
        in_specs=placed,
        out_specs=(
            P((*rows, "obj"), None),
            P(("obj", *rows), None),
            P(None, rows, "obj"),
            P((*rows, "obj")),
        ),
        check_vma=False,
    )
```

```python
import jax
import jax.numpy as jnp
from jax import lax
from jax.experimental import pallas as pl
from jax.experimental.pallas import tpu as pltpu
from jax.sharding import Mesh
from jax.sharding import PartitionSpec as P

F32 = jnp.float32
BF16 = jnp.bfloat16
LANES = 128
CHUNK = 512
GRANT = 20 * 2**20
PAIR = 2


def halves_to_lanes(rows):
    return jnp.concatenate([rows[:, :8], rows[:, 8:]], axis=2)


def lanes_to_halves(tile):
    half = tile.shape[2] // 2
    return jnp.concatenate([tile[:, :, :half], tile[:, :, half:]], axis=1)


def columns_to_rows(block):
    return jnp.concatenate(
        [block[:, c : c + LANES] for c in range(0, block.shape[1], LANES)], axis=0
    )


def by_core(block, rows):
    runs = [block[:, c : c + rows] for c in range(0, block.shape[1], rows)]
    return jnp.concatenate(runs[::2] + runs[1::2], axis=1)


def in_order(block, rows):
    half = block.shape[1] // 2
    runs = []
    for c in range(0, half, rows):
        runs += [block[:, c : c + rows], block[:, half + c : half + c + rows]]
    return jnp.concatenate(runs, axis=1)


def subject_block(subject_ref, size):
    per_owner = size // subject_ref.shape[0]
    return jnp.concatenate(
        [
            subject_ref[:, c * per_owner : (c + 1) * per_owner, :].reshape(size, LANES)
            for c in range(size // LANES)
        ],
        axis=1,
    )


def dot(a, b, contract):
    return lax.dot_general(a, b, ((contract[:1], contract[1:]), ((), ())), preferred_element_type=F32)


def pack_subject(
    subject_hbm, relation_hbm, object_hbm, out_ref, object_ref, subject_ref, relation_ref, arrived
):
    copies, _, _ = out_ref.shape
    loads = [
        pltpu.make_async_copy(subject_hbm, subject_ref, arrived.at[0]),
        pltpu.make_async_copy(relation_hbm, relation_ref, arrived.at[1]),
        pltpu.make_async_copy(object_hbm, object_ref, arrived.at[2]),
    ]
    for load in loads:
        load.start()
    for load in loads[:2]:
        load.wait()
    turned = jnp.concatenate([relation_ref[0], relation_ref[1]], axis=1).astype(F32)
    tile = halves_to_lanes(turned[None])[0].astype(BF16)
    rows = relation_ref.shape[2]
    ordered = by_core(subject_ref[...].astype(F32), rows).astype(BF16)
    factors = columns_to_rows(ordered)
    split = factors.shape[0]
    for p in range(copies):
        out_ref[p, :split] = factors
        out_ref[p, split:] = tile
    loads[2].wait()


def pack_object(gathered_ref, object_ref, out_ref):
    copies, _, width = out_ref.shape
    rows = object_ref.shape[0]
    split = gathered_ref.shape[1] - 8
    tiles = gathered_ref[:, split:, :].astype(F32)
    turned = lanes_to_halves(tiles)
    rel = turned.reshape(width, turned.shape[2]).T.astype(BF16)
    own = object_ref[...]
    for p in range(copies):
        out_ref[p, :rows] = own
        out_ref[p, rows:] = rel


def read_codes(labels_hbm, subject_ref, own_ref, sign_ref, half_ref, labels_ref, arrived):
    relations, size, _ = labels_ref.shape
    loads = [
        pltpu.make_async_copy(labels_hbm.at[k], labels_ref.at[k], arrived.at[k])
        for k in range(relations)
    ]
    for load in loads:
        load.start()
    subject = subject_block(subject_ref, size)
    half = size // 2
    ours = jnp.where(lax.axis_index("core") == 0, subject[:, :half], subject[:, half:])
    rows = size // (2 * own_ref.shape[0])
    for k in range(relations):
        half_ref[k] = dot(ours, relation_half(own_ref, k, rows), (1, 0))
    for k in range(relations):
        loads[k].wait()
        codes = labels_ref[k]
        sign_ref[k] = jnp.where(codes == 2, -1.0, jnp.where(codes > 0, 1.0, 0.0))


def relation_half(half_ref, relation, rows):
    part = half_ref[:, rows * (relation + 1) : rows * (relation + 2), :]
    return part.reshape(-1, part.shape[2])


def stacked_rows(own_ref, other_ref, part, rows):
    first = lax.axis_index("core") == 0
    own = own_ref[:, rows * part : rows * (part + 1), :]
    other = other_ref[:, rows * part : rows * (part + 1), :]
    even = jnp.where(first, own, other)
    odd = jnp.where(first, other, own)
    return jnp.stack([even, odd], axis=1).reshape(-1, own.shape[2])


def store_owners(keep_ref, send_ref, part, even, odd):
    first = lax.axis_index("core") == 0
    rows = even.shape[1]
    span = slice(rows * part, rows * (part + 1))
    keep_ref[:, span, :] = jnp.where(first, even, odd)
    send_ref[:, span, :] = jnp.where(first, odd, even)


def grads(
    subject_ref,
    own_ref,
    other_ref,
    sign_ref,
    half_ref,
    keep_ref,
    send_ref,
    carried_ref,
    signed_ref,
    left_ref,
    residual_ref,
):
    relations, size, _ = sign_ref.shape
    rows = size // (2 * keep_ref.shape[0])
    subject = subject_block(subject_ref, size)
    half = size // 2
    theirs = jnp.where(lax.axis_index("core") == 0, subject[:, half:], subject[:, :half])
    objects = stacked_rows(own_ref, other_ref, 0, rows)

    def project(k):
        rest = dot(theirs, relation_half(other_ref, k, rows), (1, 0))
        left_ref[k] = (half_ref[k] + rest).astype(BF16)

    def score(k):
        signed_ref[k] = dot(left_ref[k], objects, (1, 1))

    def settle(k):
        sign = sign_ref[k]
        signed = signed_ref[k] * sign
        small = jnp.exp(-jnp.abs(signed))
        sigmoid = jnp.where(signed >= 0.0, 1.0, small) / (1.0 + small)
        residual_ref[k] = (sigmoid * sign).astype(BF16)

    def carry(k):
        carried_ref[k] = dot(residual_ref[k], objects, (1, 0)).astype(BF16)

    def relation_grad(k):
        grad = dot(subject, carried_ref[k], (0, 0)).astype(BF16).reshape(2, -1, rows, size)
        store_owners(keep_ref, send_ref, k + 1, grad[0], grad[1])

    for k in range(relations):
        project(k)
        score(k)
        settle(k)
        if k > 0:
            relation_grad(k - 1)
        carry(k)
    relation_grad(relations - 1)
    grad_object = dot(residual_ref[0], left_ref[0], (0, 0))
    for k in range(1, relations):
        grad_object = grad_object + dot(residual_ref[k], left_ref[k], (0, 0))
    owned = grad_object.astype(BF16).reshape(-1, 2, rows, size)
    store_owners(keep_ref, send_ref, 0, owned[:, 0], owned[:, 1])


def add_pair(keep_ref, received_ref, _, out_ref):
    out_ref[...] = (keep_ref[...].astype(F32) + received_ref[...].astype(F32)).astype(BF16)


def subject_grads(
    own_ref, other_ref, signed_ref, sign_ref, carried_ref, out_ref, loss_ref, *, total
):
    relations, size, _ = signed_ref.shape
    rows = size // (2 * own_ref.shape[0])
    owners = out_ref.shape[0]
    per_owner = size // owners
    first_core = lax.axis_index("core") == 0
    rels = []
    for k in range(relations):
        own, other = relation_half(own_ref, k, rows), relation_half(other_ref, k, rows)
        even, odd = jnp.where(first_core, own, other), jnp.where(first_core, other, own)
        rels.append(jnp.concatenate([even, odd], axis=0))
    here = CHUNK // per_owner
    for at in range(0, size, CHUNK):
        span = pl.ds(at, CHUNK)
        loss = jnp.zeros((CHUNK, 1), F32)
        grad = jnp.zeros((CHUNK, size), F32)
        for k in range(relations):
            sign = sign_ref[k, span]
            signed = signed_ref[k, span] * sign
            cell = jnp.maximum(signed, 0.0) + jnp.log1p(jnp.exp(-jnp.abs(signed)))
            counted = sign != 0.0
            loss = loss + jnp.sum(jnp.where(counted, cell, 0.0), axis=1, keepdims=True)
            grad = grad + dot(carried_ref[k, span], rels[k], (1, 1))
        first = at // per_owner
        grad = grad.astype(BF16).reshape(here, per_owner, size)
        for c in range(size // LANES):
            out_ref[first : first + here, c * per_owner : (c + 1) * per_owner, :] = grad[
                :, :, c * LANES : (c + 1) * LANES
            ]
        part = jnp.broadcast_to(loss / total, (CHUNK, LANES)).reshape(here, per_owner, LANES)
        entry = lax.broadcasted_iota(jnp.int32, part.shape, 1)
        lane = lax.broadcasted_iota(jnp.int32, part.shape, 2)
        loss_ref[first : first + here] = jnp.sum(jnp.where(entry == lane, part, 0.0), axis=1)


def sum_relations(partial_ref, subject_ref, loss_ref, out_ref, *, rows):
    width = partial_ref.shape[2]
    total = jnp.sum(partial_ref[:, rows:, :].astype(F32), axis=0)
    turned = total.T
    owners, strips, _ = subject_ref.shape
    tiles = halves_to_lanes(turned.reshape(owners, width // owners, -1)).astype(BF16)
    piece = strips + 8 + PAIR
    for p in range(owners):
        at = p * piece
        out_ref[at : at + strips] = subject_ref[p]
        out_ref[at + strips : at + strips + 8] = tiles[p]
        row = jnp.broadcast_to(loss_ref[p : p + 1], (PAIR, LANES))
        out_ref[at + strips + 8 : at + piece] = row.astype(BF16)


def sum_factors(
    partial_ref, object_ref, grad_ref, grad_object_ref, relation_ref, loss_ref, *, owners, total
):
    rows, width = grad_ref.shape
    grad_object_ref[...] = jnp.sum(
        object_ref[:, : grad_object_ref.shape[0], :].astype(F32), axis=0
    )
    piece = partial_ref.shape[0] // owners
    summed = partial_ref[:piece].astype(F32)
    for p in range(1, owners):
        summed = summed + partial_ref[p * piece : (p + 1) * piece].astype(F32)
    blocks = width // LANES
    grad = jnp.concatenate([summed[c * rows : (c + 1) * rows] for c in range(blocks)], axis=1)
    grad_ref[...] = in_order(grad, relation_ref.shape[2])
    at = blocks * rows
    turned = lanes_to_halves(summed[None, at : at + 8])[0] * (1.0 / total)
    columns = relation_ref.shape[2]
    for k in range(relation_ref.shape[0]):
        relation_ref[k] = turned[:, k * columns : (k + 1) * columns]
    loss_ref[...] = summed[at + 8 : at + 9, :rows]


def shape(dims, dtype=BF16):
    return jax.ShapeDtypeStruct(dims, dtype)


def call(kernel, name, outs, *args, scratch=(), spaces=None):
    spaces = spaces or [None] * len(args)
    args = [
        pltpu.with_memory_space_constraint(a, s) if s is pltpu.HBM else a
        for a, s in zip(args, spaces)
    ]
    return pl.pallas_call(
        kernel,
        out_shape=outs,
        in_specs=[pl.BlockSpec(memory_space=space) for space in spaces],
        scratch_shapes=scratch,
        name=name,
        compiler_params=pltpu.CompilerParams(vmem_limit_bytes=GRANT),
    )(*args)


def to_other_core(array):
    return lax.ppermute(array, "core", [(0, 1), (1, 0)])


def body(subject_factors, object_factors, relations, labels):
    chips, obj = lax.axis_size("chip"), lax.axis_size("obj")
    subj = 2 * chips
    subject_rows, width = subject_factors.shape
    object_part = object_factors.shape[0]
    count, rel_rows, rel_columns = relations.shape
    _, subjects, objects = labels.shape
    strips = width // LANES * subject_rows
    turned = jnp.swapaxes(relations, 1, 2)
    sent, object_own = call(
        pack_subject,
        "pack_subject",
        (shape((obj, strips + 8, LANES)), shape(object_factors.shape)),
        subject_factors,
        turned,
        object_factors,
        scratch=[
            pltpu.VMEM(subject_factors.shape, BF16),
            pltpu.VMEM(turned.shape, BF16),
            pltpu.SemaphoreType.DMA((3,)),
        ],
        spaces=[pltpu.HBM] * 3,
    )
    subject_all = lax.all_to_all(sent, "obj", 0, 0, tiled=True)
    stacked = (chips, object_part + count * rel_rows, width)
    sent = call(pack_object, "pack_object", shape(stacked), subject_all, object_own)
    own = lax.all_to_all(sent, "chip", 0, 0, tiled=True)
    other = to_other_core(own)
    square = (count, subjects, width)
    sign, half = call(
        read_codes,
        "read_codes",
        (shape(labels.shape, F32), shape(square, F32)),
        labels,
        subject_all,
        own,
        scratch=[pltpu.VMEM(labels.shape, labels.dtype), pltpu.SemaphoreType.DMA((count,))],
        spaces=[pltpu.HBM, None, None],
    )
    keep, send, carried, signed = call(
        grads,
        "grads",
        (shape(stacked), shape(stacked), shape(square), shape(labels.shape, F32)),
        subject_all,
        own,
        other,
        sign,
        half,
        scratch=[pltpu.VMEM(square, BF16), pltpu.VMEM(labels.shape, BF16)],
    )
    swapped = to_other_core(send)
    scale = float(count * objects * obj)
    packed, loss_rows = call(
        lambda *refs: subject_grads(*refs, total=scale),
        "subject_grads",
        (shape((obj, strips, LANES)), shape((obj, LANES), F32)),
        own,
        other,
        signed,
        sign,
        carried,
    )
    sent = call(
        add_pair,
        "add_pair",
        shape(stacked),
        keep,
        swapped,
        packed,
        spaces=[None, None, pl.ANY],
    )
    object_partial = lax.all_to_all(sent, "chip", 0, 0, tiled=True)
    piece = strips + 8 + PAIR
    sent = call(
        lambda *refs: sum_relations(*refs, rows=object_part),
        "sum_relations",
        shape((obj * piece, LANES)),
        object_partial,
        packed,
        loss_rows,
    )
    sent = sent.reshape(-1, PAIR, LANES)
    received = lax.all_to_all(sent, "obj", 0, 0, tiled=True).reshape(-1, LANES)
    scale = float(subjects * subj)
    grad_subject, grad_object, grad_relations, loss = call(
        lambda *refs: sum_factors(*refs, owners=obj, total=scale),
        "sum_factors",
        (
            shape((subject_rows, width), F32),
            shape((object_part, width), F32),
            shape((count, rel_columns, rel_rows), F32),
            shape((1, subject_rows), F32),
        ),
        received,
        object_partial,
    )
    return grad_subject, grad_object, jnp.swapaxes(grad_relations, 1, 2), loss.reshape(subject_rows)


def solution(mesh):
    subj, obj = mesh.shape["subj"], mesh.shape["obj"]
    cores = Mesh(mesh.devices.reshape(subj // 2, 2, obj), ("chip", "core", "obj"))
    rows = ("chip", "core")
    placed = (
        P((*rows, "obj"), None),
        P(("obj", *rows), None),
        P(None, rows, "obj"),
        P(None, rows, "obj"),
    )
    return jax.shard_map(
        body,
        mesh=cores,
        in_specs=placed,
        out_specs=(
            P((*rows, "obj"), None),
            P(("obj", *rows), None),
            P(None, rows, "obj"),
            P((*rows, "obj")),
        ),
        check_vma=False,
    )
```

```python
import jax
import jax.numpy as jnp
from jax import lax
from jax.experimental import pallas as pl
from jax.experimental.pallas import tpu as pltpu
from jax.sharding import Mesh
from jax.sharding import PartitionSpec as P

F32 = jnp.float32
BF16 = jnp.bfloat16
LANES = 128
CHUNK = 512
GRANT = 20 * 2**20
PAIR = 2


def halves_to_lanes(rows):
    return jnp.concatenate([rows[:, :8], rows[:, 8:]], axis=2)


def lanes_to_halves(tile):
    half = tile.shape[2] // 2
    return jnp.concatenate([tile[:, :, :half], tile[:, :, half:]], axis=1)


def columns_to_rows(block):
    return jnp.concatenate(
        [block[:, c : c + LANES] for c in range(0, block.shape[1], LANES)], axis=0
    )


def by_core(block, rows):
    runs = [block[:, c : c + rows] for c in range(0, block.shape[1], rows)]
    return jnp.concatenate(runs[::2] + runs[1::2], axis=1)


def in_order(block, rows):
    half = block.shape[1] // 2
    runs = []
    for c in range(0, half, rows):
        runs += [block[:, c : c + rows], block[:, half + c : half + c + rows]]
    return jnp.concatenate(runs, axis=1)


def subject_block(subject_ref, size):
    per_owner = size // subject_ref.shape[0]
    return jnp.concatenate(
        [
            subject_ref[:, c * per_owner : (c + 1) * per_owner, :].reshape(size, LANES)
            for c in range(size // LANES)
        ],
        axis=1,
    )


def dot(a, b, contract):
    return lax.dot_general(a, b, ((contract[:1], contract[1:]), ((), ())), preferred_element_type=F32)


def pack_subject(
    subject_hbm, relation_hbm, object_hbm, out_ref, object_ref, subject_ref, relation_ref, arrived
):
    copies, _, _ = out_ref.shape
    loads = [
        pltpu.make_async_copy(subject_hbm, subject_ref, arrived.at[0]),
        pltpu.make_async_copy(relation_hbm, relation_ref, arrived.at[1]),
        pltpu.make_async_copy(object_hbm, object_ref, arrived.at[2]),
    ]
    for load in loads:
        load.start()
    for load in loads[:2]:
        load.wait()
    turned = jnp.concatenate([relation_ref[0], relation_ref[1]], axis=1).astype(F32)
    tile = halves_to_lanes(turned[None])[0].astype(BF16)
    rows = relation_ref.shape[2]
    ordered = by_core(subject_ref[...].astype(F32), rows).astype(BF16)
    factors = columns_to_rows(ordered)
    split = factors.shape[0]
    for p in range(copies):
        out_ref[p, :split] = factors
        out_ref[p, split:] = tile
    loads[2].wait()


def pack_object(gathered_ref, object_ref, out_ref):
    copies, _, width = out_ref.shape
    rows = object_ref.shape[0]
    split = gathered_ref.shape[1] - 8
    tiles = gathered_ref[:, split:, :].astype(F32)
    turned = lanes_to_halves(tiles)
    rel = turned.reshape(width, turned.shape[2]).T.astype(BF16)
    own = object_ref[...]
    for p in range(copies):
        out_ref[p, :rows] = own
        out_ref[p, rows:] = rel


def read_codes(
    labels_hbm, subject_ref, own_ref, sign_ref, half_ref, turned_ref, labels_ref, arrived
):
    relations, size, _ = labels_ref.shape
    loads = [
        pltpu.make_async_copy(labels_hbm.at[k], labels_ref.at[k], arrived.at[k])
        for k in range(relations)
    ]
    for load in loads:
        load.start()
    subject = subject_block(subject_ref, size)
    half = size // 2
    ours = jnp.where(lax.axis_index("core") == 0, subject[:, :half], subject[:, half:])
    rows = size // (2 * own_ref.shape[0])
    for k in range(relations):
        half_ref[k] = dot(ours, relation_half(own_ref, k, rows), (1, 0))
    turned_ref[...] = subject.T
    for k in range(relations):
        loads[k].wait()
        codes = labels_ref[k]
        sign_ref[k] = jnp.where(codes == 2, -1.0, jnp.where(codes > 0, 1.0, 0.0))


def relation_half(half_ref, relation, rows):
    part = half_ref[:, rows * (relation + 1) : rows * (relation + 2), :]
    return part.reshape(-1, part.shape[2])


def stacked_rows(own_ref, other_ref, part, rows):
    first = lax.axis_index("core") == 0
    own = own_ref[:, rows * part : rows * (part + 1), :]
    other = other_ref[:, rows * part : rows * (part + 1), :]
    even = jnp.where(first, own, other)
    odd = jnp.where(first, other, own)
    return jnp.stack([even, odd], axis=1).reshape(-1, own.shape[2])


def store_owners(keep_ref, send_ref, part, even, odd):
    first = lax.axis_index("core") == 0
    rows = even.shape[1]
    span = slice(rows * part, rows * (part + 1))
    keep_ref[:, span, :] = jnp.where(first, even, odd)
    send_ref[:, span, :] = jnp.where(first, odd, even)


def grads(
    subject_ref,
    own_ref,
    other_ref,
    sign_ref,
    half_ref,
    turned_ref,
    keep_ref,
    send_ref,
    carried_ref,
    signed_ref,
    left_ref,
    residual_ref,
):
    relations, size, _ = sign_ref.shape
    rows = size // (2 * keep_ref.shape[0])
    subject = subject_block(subject_ref, size)
    half = size // 2
    theirs = jnp.where(lax.axis_index("core") == 0, subject[:, half:], subject[:, :half])
    objects = stacked_rows(own_ref, other_ref, 0, rows)

    def project(k):
        rest = dot(theirs, relation_half(other_ref, k, rows), (1, 0))
        left_ref[k] = (half_ref[k] + rest).astype(BF16)

    def score(k):
        signed_ref[k] = dot(left_ref[k], objects, (1, 1))

    def settle(k):
        sign = sign_ref[k]
        signed = signed_ref[k] * sign
        small = jnp.exp(-jnp.abs(signed))
        sigmoid = jnp.where(signed >= 0.0, 1.0, small) / (1.0 + small)
        residual_ref[k] = (sigmoid * sign).astype(BF16)

    def carry(k):
        carried_ref[k] = dot(residual_ref[k], objects, (1, 0)).astype(BF16)

    def relation_grad(k):
        grad = dot(turned_ref[...], carried_ref[k], (1, 0)).astype(BF16).reshape(2, -1, rows, size)
        store_owners(keep_ref, send_ref, k + 1, grad[0], grad[1])

    project(0)
    score(0)
    for k in range(relations):
        more = k + 1 < relations
        if more:
            project(k + 1)
        settle(k)
        if more:
            score(k + 1)
        if k > 0:
            relation_grad(k - 1)
        carry(k)
    relation_grad(relations - 1)
    grad_object = dot(residual_ref[0], left_ref[0], (0, 0))
    for k in range(1, relations):
        grad_object = grad_object + dot(residual_ref[k], left_ref[k], (0, 0))
    owned = grad_object.astype(BF16).reshape(-1, 2, rows, size)
    store_owners(keep_ref, send_ref, 0, owned[:, 0], owned[:, 1])


def add_pair(keep_ref, received_ref, _, out_ref):
    out_ref[...] = (keep_ref[...].astype(F32) + received_ref[...].astype(F32)).astype(BF16)


def subject_grads(
    own_ref, other_ref, signed_ref, sign_ref, carried_ref, out_ref, loss_ref, *, total
):
    relations, size, _ = signed_ref.shape
    rows = size // (2 * own_ref.shape[0])
    owners = out_ref.shape[0]
    per_owner = size // owners
    first_core = lax.axis_index("core") == 0
    rels = []
    for k in range(relations):
        own, other = relation_half(own_ref, k, rows), relation_half(other_ref, k, rows)
        even, odd = jnp.where(first_core, own, other), jnp.where(first_core, other, own)
        rels.append(jnp.concatenate([even, odd], axis=0))
    here = CHUNK // per_owner
    for at in range(0, size, CHUNK):
        span = pl.ds(at, CHUNK)
        loss = jnp.zeros((CHUNK, 1), F32)
        grad = jnp.zeros((CHUNK, size), F32)
        for k in range(relations):
            sign = sign_ref[k, span]
            signed = signed_ref[k, span] * sign
            cell = jnp.maximum(signed, 0.0) + jnp.log1p(jnp.exp(-jnp.abs(signed)))
            counted = sign != 0.0
            loss = loss + jnp.sum(jnp.where(counted, cell, 0.0), axis=1, keepdims=True)
            grad = grad + dot(carried_ref[k, span], rels[k], (1, 1))
        first = at // per_owner
        grad = grad.astype(BF16).reshape(here, per_owner, size)
        for c in range(size // LANES):
            out_ref[first : first + here, c * per_owner : (c + 1) * per_owner, :] = grad[
                :, :, c * LANES : (c + 1) * LANES
            ]
        part = jnp.broadcast_to(loss / total, (CHUNK, LANES)).reshape(here, per_owner, LANES)
        entry = lax.broadcasted_iota(jnp.int32, part.shape, 1)
        lane = lax.broadcasted_iota(jnp.int32, part.shape, 2)
        loss_ref[first : first + here] = jnp.sum(jnp.where(entry == lane, part, 0.0), axis=1)


def sum_relations(partial_ref, subject_ref, loss_ref, out_ref, *, rows):
    width = partial_ref.shape[2]
    total = jnp.sum(partial_ref[:, rows:, :].astype(F32), axis=0)
    turned = total.T
    owners, strips, _ = subject_ref.shape
    tiles = halves_to_lanes(turned.reshape(owners, width // owners, -1)).astype(BF16)
    piece = strips + 8 + PAIR
    for p in range(owners):
        at = p * piece
        out_ref[at : at + strips] = subject_ref[p]
        out_ref[at + strips : at + strips + 8] = tiles[p]
        row = jnp.broadcast_to(loss_ref[p : p + 1], (PAIR, LANES))
        out_ref[at + strips + 8 : at + piece] = row.astype(BF16)


def sum_factors(
    partial_ref, object_ref, grad_ref, grad_object_ref, relation_ref, loss_ref, *, owners, total
):
    rows, width = grad_ref.shape
    grad_object_ref[...] = jnp.sum(
        object_ref[:, : grad_object_ref.shape[0], :].astype(F32), axis=0
    )
    piece = partial_ref.shape[0] // owners
    summed = partial_ref[:piece].astype(F32)
    for p in range(1, owners):
        summed = summed + partial_ref[p * piece : (p + 1) * piece].astype(F32)
    blocks = width // LANES
    grad = jnp.concatenate([summed[c * rows : (c + 1) * rows] for c in range(blocks)], axis=1)
    grad_ref[...] = in_order(grad, relation_ref.shape[2])
    at = blocks * rows
    turned = lanes_to_halves(summed[None, at : at + 8])[0] * (1.0 / total)
    columns = relation_ref.shape[2]
    for k in range(relation_ref.shape[0]):
        relation_ref[k] = turned[:, k * columns : (k + 1) * columns]
    loss_ref[...] = summed[at + 8 : at + 9, :rows]


def shape(dims, dtype=BF16):
    return jax.ShapeDtypeStruct(dims, dtype)


def call(kernel, name, outs, *args, scratch=(), spaces=None):
    spaces = spaces or [None] * len(args)
    args = [
        pltpu.with_memory_space_constraint(a, s) if s is pltpu.HBM else a
        for a, s in zip(args, spaces)
    ]
    return pl.pallas_call(
        kernel,
        out_shape=outs,
        in_specs=[pl.BlockSpec(memory_space=space) for space in spaces],
        scratch_shapes=scratch,
        name=name,
        compiler_params=pltpu.CompilerParams(vmem_limit_bytes=GRANT),
    )(*args)


def to_other_core(array):
    return lax.ppermute(array, "core", [(0, 1), (1, 0)])


def body(subject_factors, object_factors, relations, labels):
    chips, obj = lax.axis_size("chip"), lax.axis_size("obj")
    subj = 2 * chips
    subject_rows, width = subject_factors.shape
    object_part = object_factors.shape[0]
    count, rel_rows, rel_columns = relations.shape
    _, subjects, objects = labels.shape
    strips = width // LANES * subject_rows
    turned = jnp.swapaxes(relations, 1, 2)
    sent, object_own = call(
        pack_subject,
        "pack_subject",
        (shape((obj, strips + 8, LANES)), shape(object_factors.shape)),
        subject_factors,
        turned,
        object_factors,
        scratch=[
            pltpu.VMEM(subject_factors.shape, BF16),
            pltpu.VMEM(turned.shape, BF16),
            pltpu.SemaphoreType.DMA((3,)),
        ],
        spaces=[pltpu.HBM] * 3,
    )
    subject_all = lax.all_to_all(sent, "obj", 0, 0, tiled=True)
    stacked = (chips, object_part + count * rel_rows, width)
    sent = call(pack_object, "pack_object", shape(stacked), subject_all, object_own)
    own = lax.all_to_all(sent, "chip", 0, 0, tiled=True)
    other = to_other_core(own)
    square = (count, subjects, width)
    sign, half, transposed = call(
        read_codes,
        "read_codes",
        (shape(labels.shape, F32), shape(square, F32), shape((width, subjects))),
        labels,
        subject_all,
        own,
        scratch=[pltpu.VMEM(labels.shape, labels.dtype), pltpu.SemaphoreType.DMA((count,))],
        spaces=[pltpu.HBM, None, None],
    )
    keep, send, carried, signed = call(
        grads,
        "grads",
        (shape(stacked), shape(stacked), shape(square), shape(labels.shape, F32)),
        subject_all,
        own,
        other,
        sign,
        half,
        transposed,
        scratch=[pltpu.VMEM(square, BF16), pltpu.VMEM(labels.shape, BF16)],
    )
    swapped = to_other_core(send)
    scale = float(count * objects * obj)
    packed, loss_rows = call(
        lambda *refs: subject_grads(*refs, total=scale),
        "subject_grads",
        (shape((obj, strips, LANES)), shape((obj, LANES), F32)),
        own,
        other,
        signed,
        sign,
        carried,
    )
    sent = call(
        add_pair,
        "add_pair",
        shape(stacked),
        keep,
        swapped,
        packed,
        spaces=[None, None, pl.ANY],
    )
    object_partial = lax.all_to_all(sent, "chip", 0, 0, tiled=True)
    piece = strips + 8 + PAIR
    sent = call(
        lambda *refs: sum_relations(*refs, rows=object_part),
        "sum_relations",
        shape((obj * piece, LANES)),
        object_partial,
        packed,
        loss_rows,
    )
    sent = sent.reshape(-1, PAIR, LANES)
    received = lax.all_to_all(sent, "obj", 0, 0, tiled=True).reshape(-1, LANES)
    scale = float(subjects * subj)
    grad_subject, grad_object, grad_relations, loss = call(
        lambda *refs: sum_factors(*refs, owners=obj, total=scale),
        "sum_factors",
        (
            shape((subject_rows, width), F32),
            shape((object_part, width), F32),
            shape((count, rel_columns, rel_rows), F32),
            shape((1, subject_rows), F32),
        ),
        received,
        object_partial,
    )
    return grad_subject, grad_object, jnp.swapaxes(grad_relations, 1, 2), loss.reshape(subject_rows)


def solution(mesh):
    subj, obj = mesh.shape["subj"], mesh.shape["obj"]
    cores = Mesh(mesh.devices.reshape(subj // 2, 2, obj), ("chip", "core", "obj"))
    rows = ("chip", "core")
    placed = (
        P((*rows, "obj"), None),
        P(("obj", *rows), None),
        P(None, rows, "obj"),
        P(None, rows, "obj"),
    )
    return jax.shard_map(
        body,
        mesh=cores,
        in_specs=placed,
        out_specs=(
            P((*rows, "obj"), None),
            P(("obj", *rows), None),
            P(None, rows, "obj"),
            P((*rows, "obj")),
        ),
        check_vma=False,
    )
```

```python
import jax
import jax.numpy as jnp
from jax import lax
from jax.experimental import pallas as pl
from jax.experimental.pallas import tpu as pltpu
from jax.sharding import Mesh
from jax.sharding import PartitionSpec as P

F32 = jnp.float32
BF16 = jnp.bfloat16
LANES = 128
CHUNK = 512
GRANT = 20 * 2**20
PAIR = 2


def halves_to_lanes(rows):
    return jnp.concatenate([rows[:, :8], rows[:, 8:]], axis=2)


def lanes_to_halves(tile):
    half = tile.shape[2] // 2
    return jnp.concatenate([tile[:, :, :half], tile[:, :, half:]], axis=1)


def columns_to_rows(block):
    return jnp.concatenate(
        [block[:, c : c + LANES] for c in range(0, block.shape[1], LANES)], axis=0
    )


def by_core(block, rows):
    runs = [block[:, c : c + rows] for c in range(0, block.shape[1], rows)]
    return jnp.concatenate(runs[::2] + runs[1::2], axis=1)


def in_order(block, rows):
    half = block.shape[1] // 2
    runs = []
    for c in range(0, half, rows):
        runs += [block[:, c : c + rows], block[:, half + c : half + c + rows]]
    return jnp.concatenate(runs, axis=1)


def subject_block(subject_ref, size):
    per_owner = size // subject_ref.shape[0]
    return jnp.concatenate(
        [
            subject_ref[:, c * per_owner : (c + 1) * per_owner, :].reshape(size, LANES)
            for c in range(size // LANES)
        ],
        axis=1,
    )


def dot(a, b, contract):
    return lax.dot_general(a, b, ((contract[:1], contract[1:]), ((), ())), preferred_element_type=F32)


def pack_subject(
    subject_hbm, relation_hbm, object_hbm, out_ref, object_ref, subject_ref, relation_ref, arrived
):
    copies, _, _ = out_ref.shape
    loads = [
        pltpu.make_async_copy(subject_hbm, subject_ref, arrived.at[0]),
        pltpu.make_async_copy(relation_hbm, relation_ref, arrived.at[1]),
        pltpu.make_async_copy(object_hbm, object_ref, arrived.at[2]),
    ]
    for load in loads:
        load.start()
    for load in loads[:2]:
        load.wait()
    turned = jnp.concatenate([relation_ref[0], relation_ref[1]], axis=1).astype(F32)
    tile = halves_to_lanes(turned[None])[0].astype(BF16)
    rows = relation_ref.shape[2]
    ordered = by_core(subject_ref[...].astype(F32), rows).astype(BF16)
    factors = columns_to_rows(ordered)
    split = factors.shape[0]
    for p in range(copies):
        out_ref[p, :split] = factors
        out_ref[p, split:] = tile
    loads[2].wait()


def pack_object(gathered_ref, object_ref, out_ref):
    copies, _, width = out_ref.shape
    rows = object_ref.shape[0]
    split = gathered_ref.shape[1] - 8
    tiles = gathered_ref[:, split:, :].astype(F32)
    turned = lanes_to_halves(tiles)
    rel = turned.reshape(width, turned.shape[2]).T.astype(BF16)
    own = object_ref[...]
    for p in range(copies):
        out_ref[p, :rows] = own
        out_ref[p, rows:] = rel


def read_codes(
    labels_hbm, subject_ref, own_ref, sign_ref, half_ref, turned_ref, labels_ref, arrived
):
    relations, size, _ = labels_ref.shape
    loads = [
        pltpu.make_async_copy(labels_hbm.at[k], labels_ref.at[k], arrived.at[k])
        for k in range(relations)
    ]
    for load in loads:
        load.start()
    subject = subject_block(subject_ref, size)
    half = size // 2
    ours = jnp.where(lax.axis_index("core") == 0, subject[:, :half], subject[:, half:])
    rows = size // (2 * own_ref.shape[0])
    for k in range(relations):
        half_ref[k] = dot(ours, relation_half(own_ref, k, rows), (1, 0))
    turned_ref[...] = subject.T
    for k in range(relations):
        loads[k].wait()
        codes = labels_ref[k]
        sign_ref[k] = jnp.where(codes == 2, -1.0, jnp.where(codes > 0, 1.0, 0.0))


def relation_half(half_ref, relation, rows):
    part = half_ref[:, rows * (relation + 1) : rows * (relation + 2), :]
    return part.reshape(-1, part.shape[2])


def stacked_rows(own_ref, other_ref, part, rows):
    first = lax.axis_index("core") == 0
    own = own_ref[:, rows * part : rows * (part + 1), :]
    other = other_ref[:, rows * part : rows * (part + 1), :]
    even = jnp.where(first, own, other)
    odd = jnp.where(first, other, own)
    return jnp.stack([even, odd], axis=1).reshape(-1, own.shape[2])


def store_owners(keep_ref, send_ref, part, even, odd):
    first = lax.axis_index("core") == 0
    rows = even.shape[1]
    span = slice(rows * part, rows * (part + 1))
    keep_ref[:, span, :] = jnp.where(first, even, odd)
    send_ref[:, span, :] = jnp.where(first, odd, even)


def grads(
    subject_ref,
    own_ref,
    other_ref,
    sign_ref,
    half_ref,
    turned_ref,
    keep_ref,
    send_ref,
    carried_ref,
    signed_ref,
    left_ref,
    residual_ref,
):
    relations, size, _ = sign_ref.shape
    rows = size // (2 * keep_ref.shape[0])
    subject = subject_block(subject_ref, size)
    half = size // 2
    theirs = jnp.where(lax.axis_index("core") == 0, subject[:, half:], subject[:, :half])
    objects = stacked_rows(own_ref, other_ref, 0, rows)

    def project(k):
        rest = dot(theirs, relation_half(other_ref, k, rows), (1, 0))
        left_ref[k] = (half_ref[k] + rest).astype(BF16)

    def score(k):
        signed_ref[k] = dot(left_ref[k], objects, (1, 1))

    def settle(k):
        sign = sign_ref[k]
        signed = signed_ref[k] * sign
        small = jnp.exp(-jnp.abs(signed))
        sigmoid = jnp.where(signed >= 0.0, 1.0, small) / (1.0 + small)
        residual_ref[k] = (sigmoid * sign).astype(BF16)

    def carry(k):
        carried_ref[k] = dot(residual_ref[k], objects, (1, 0)).astype(BF16)

    def relation_grad(k):
        grad = dot(turned_ref[...], carried_ref[k], (1, 0)).astype(BF16).reshape(2, -1, rows, size)
        store_owners(keep_ref, send_ref, k + 1, grad[0], grad[1])

    project(0)
    score(0)
    for k in range(relations):
        more = k + 1 < relations
        if more:
            project(k + 1)
        settle(k)
        if more:
            score(k + 1)
        if k > 0:
            relation_grad(k - 1)
        carry(k)
    relation_grad(relations - 1)
    grad_object = dot(residual_ref[0], left_ref[0], (0, 0))
    for k in range(1, relations):
        grad_object = grad_object + dot(residual_ref[k], left_ref[k], (0, 0))
    owned = grad_object.astype(BF16).reshape(-1, 2, rows, size)
    store_owners(keep_ref, send_ref, 0, owned[:, 0], owned[:, 1])


def add_pair(keep_ref, received_ref, _, out_ref):
    out_ref[...] = keep_ref[...] + received_ref[...]


def subject_grads(
    own_ref, other_ref, signed_ref, sign_ref, carried_ref, out_ref, loss_ref, *, total
):
    relations, size, _ = signed_ref.shape
    rows = size // (2 * own_ref.shape[0])
    owners = out_ref.shape[0]
    per_owner = size // owners
    first_core = lax.axis_index("core") == 0
    rels = []
    for k in range(relations):
        own, other = relation_half(own_ref, k, rows), relation_half(other_ref, k, rows)
        even, odd = jnp.where(first_core, own, other), jnp.where(first_core, other, own)
        rels.append(jnp.concatenate([even, odd], axis=0))
    here = CHUNK // per_owner
    for at in range(0, size, CHUNK):
        span = pl.ds(at, CHUNK)
        loss = jnp.zeros((CHUNK, 1), F32)
        grad = jnp.zeros((CHUNK, size), F32)
        for k in range(relations):
            sign = sign_ref[k, span]
            signed = signed_ref[k, span] * sign
            cell = jnp.maximum(signed, 0.0) + jnp.log1p(jnp.exp(-jnp.abs(signed)))
            counted = sign != 0.0
            loss = loss + jnp.sum(jnp.where(counted, cell, 0.0), axis=1, keepdims=True)
            grad = grad + dot(carried_ref[k, span], rels[k], (1, 1))
        first = at // per_owner
        grad = grad.astype(BF16).reshape(here, per_owner, size)
        for c in range(size // LANES):
            out_ref[first : first + here, c * per_owner : (c + 1) * per_owner, :] = grad[
                :, :, c * LANES : (c + 1) * LANES
            ]
        part = jnp.broadcast_to(loss / total, (CHUNK, LANES)).reshape(here, per_owner, LANES)
        entry = lax.broadcasted_iota(jnp.int32, part.shape, 1)
        lane = lax.broadcasted_iota(jnp.int32, part.shape, 2)
        loss_ref[first : first + here] = jnp.sum(jnp.where(entry == lane, part, 0.0), axis=1)


def sum_relations(partial_ref, subject_ref, loss_ref, out_ref, *, rows):
    width = partial_ref.shape[2]
    total = jnp.sum(partial_ref[:, rows:, :].astype(F32), axis=0)
    turned = total.T
    owners, strips, _ = subject_ref.shape
    tiles = halves_to_lanes(turned.reshape(owners, width // owners, -1)).astype(BF16)
    piece = strips + 8 + PAIR
    for p in range(owners):
        at = p * piece
        out_ref[at : at + strips] = subject_ref[p]
        out_ref[at + strips : at + strips + 8] = tiles[p]
        row = jnp.broadcast_to(loss_ref[p : p + 1], (PAIR, LANES))
        out_ref[at + strips + 8 : at + piece] = row.astype(BF16)


def sum_factors(
    partial_ref, object_ref, grad_ref, grad_object_ref, relation_ref, loss_ref, *, owners, total
):
    rows, width = grad_ref.shape
    grad_object_ref[...] = jnp.sum(
        object_ref[:, : grad_object_ref.shape[0], :].astype(F32), axis=0
    )
    piece = partial_ref.shape[0] // owners
    summed = partial_ref[:piece].astype(F32)
    for p in range(1, owners):
        summed = summed + partial_ref[p * piece : (p + 1) * piece].astype(F32)
    blocks = width // LANES
    grad = jnp.concatenate([summed[c * rows : (c + 1) * rows] for c in range(blocks)], axis=1)
    grad_ref[...] = in_order(grad, relation_ref.shape[2])
    at = blocks * rows
    turned = lanes_to_halves(summed[None, at : at + 8])[0] * (1.0 / total)
    columns = relation_ref.shape[2]
    for k in range(relation_ref.shape[0]):
        relation_ref[k] = turned[:, k * columns : (k + 1) * columns]
    loss_ref[...] = summed[at + 8 : at + 9, :rows]


def shape(dims, dtype=BF16):
    return jax.ShapeDtypeStruct(dims, dtype)


def call(kernel, name, outs, *args, scratch=(), spaces=None):
    spaces = spaces or [None] * len(args)
    args = [
        pltpu.with_memory_space_constraint(a, s) if s is pltpu.HBM else a
        for a, s in zip(args, spaces)
    ]
    return pl.pallas_call(
        kernel,
        out_shape=outs,
        in_specs=[pl.BlockSpec(memory_space=space) for space in spaces],
        scratch_shapes=scratch,
        name=name,
        compiler_params=pltpu.CompilerParams(vmem_limit_bytes=GRANT),
    )(*args)


def to_other_core(array):
    return lax.ppermute(array, "core", [(0, 1), (1, 0)])


def body(subject_factors, object_factors, relations, labels):
    chips, obj = lax.axis_size("chip"), lax.axis_size("obj")
    subj = 2 * chips
    subject_rows, width = subject_factors.shape
    object_part = object_factors.shape[0]
    count, rel_rows, rel_columns = relations.shape
    _, subjects, objects = labels.shape
    strips = width // LANES * subject_rows
    turned = jnp.swapaxes(relations, 1, 2)
    sent, object_own = call(
        pack_subject,
        "pack_subject",
        (shape((obj, strips + 8, LANES)), shape(object_factors.shape)),
        subject_factors,
        turned,
        object_factors,
        scratch=[
            pltpu.VMEM(subject_factors.shape, BF16),
            pltpu.VMEM(turned.shape, BF16),
            pltpu.SemaphoreType.DMA((3,)),
        ],
        spaces=[pltpu.HBM] * 3,
    )
    subject_all = lax.all_to_all(sent, "obj", 0, 0, tiled=True)
    stacked = (chips, object_part + count * rel_rows, width)
    sent = call(pack_object, "pack_object", shape(stacked), subject_all, object_own)
    own = lax.all_to_all(sent, "chip", 0, 0, tiled=True)
    other = to_other_core(own)
    square = (count, subjects, width)
    sign, half, transposed = call(
        read_codes,
        "read_codes",
        (shape(labels.shape, F32), shape(square, F32), shape((width, subjects))),
        labels,
        subject_all,
        own,
        scratch=[pltpu.VMEM(labels.shape, labels.dtype), pltpu.SemaphoreType.DMA((count,))],
        spaces=[pltpu.HBM, None, None],
    )
    keep, send, carried, signed = call(
        grads,
        "grads",
        (shape(stacked), shape(stacked), shape(square), shape(labels.shape, F32)),
        subject_all,
        own,
        other,
        sign,
        half,
        transposed,
        scratch=[pltpu.VMEM(square, BF16), pltpu.VMEM(labels.shape, BF16)],
    )
    swapped = to_other_core(send)
    scale = float(count * objects * obj)
    packed, loss_rows = call(
        lambda *refs: subject_grads(*refs, total=scale),
        "subject_grads",
        (shape((obj, strips, LANES)), shape((obj, LANES), F32)),
        own,
        other,
        signed,
        sign,
        carried,
    )
    sent = call(
        add_pair,
        "add_pair",
        shape(stacked),
        keep,
        swapped,
        packed,
        spaces=[None, None, pl.ANY],
    )
    object_partial = lax.all_to_all(sent, "chip", 0, 0, tiled=True)
    piece = strips + 8 + PAIR
    sent = call(
        lambda *refs: sum_relations(*refs, rows=object_part),
        "sum_relations",
        shape((obj * piece, LANES)),
        object_partial,
        packed,
        loss_rows,
    )
    sent = sent.reshape(-1, PAIR, LANES)
    received = lax.all_to_all(sent, "obj", 0, 0, tiled=True).reshape(-1, LANES)
    scale = float(subjects * subj)
    grad_subject, grad_object, grad_relations, loss = call(
        lambda *refs: sum_factors(*refs, owners=obj, total=scale),
        "sum_factors",
        (
            shape((subject_rows, width), F32),
            shape((object_part, width), F32),
            shape((count, rel_columns, rel_rows), F32),
            shape((1, subject_rows), F32),
        ),
        received,
        object_partial,
    )
    return grad_subject, grad_object, jnp.swapaxes(grad_relations, 1, 2), loss.reshape(subject_rows)


def solution(mesh):
    subj, obj = mesh.shape["subj"], mesh.shape["obj"]
    cores = Mesh(mesh.devices.reshape(subj // 2, 2, obj), ("chip", "core", "obj"))
    rows = ("chip", "core")
    placed = (
        P((*rows, "obj"), None),
        P(("obj", *rows), None),
        P(None, rows, "obj"),
        P(None, rows, "obj"),
    )
    return jax.shard_map(
        body,
        mesh=cores,
        in_specs=placed,
        out_specs=(
            P((*rows, "obj"), None),
            P(("obj", *rows), None),
            P(None, rows, "obj"),
            P((*rows, "obj")),
        ),
        check_vma=False,
    )
```
